128 devices in a mesh: center: 16 (over y, x), expert: 8 (over z, core).
Axes of the slice: x: 4, y: 4, z: 4, core: 2. Of those that a mesh axis runs over, the one named last changes fastest.
Arguments:
- tokens: bfloat16 [16384, 2048], P(('center', 'expert')), may hold values from -6 to 6
- doc_ids: int32 [128, 128], P(('center', 'expert')), may hold values from 0 to 7, never falling along the last dimension, each value on 1 to 32 neighbouring positions
- expert_ids: int32 [16384, 8], P(('center', 'expert')), may hold values from 0 to 127, all different within a row; in each aligned block of 128 rows (0 to 127, 128 to 255, ...) at most 16 rows name the same one
- gate_raw: float32 [16384, 8], P(('center', 'expert')), may hold values from 0.1 to 1
- gate_up: bfloat16 [128, 2048, 1536], P(('center', 'expert')), may hold values from -0.125 to 0.125
- down: bfloat16 [128, 768, 2048], P(('center', 'expert'))
- bank: bfloat16 [32768, 2048], P('center')
Outputs:
- layer_out: bfloat16 [16384, 2048], P(('center', 'expert'))
- scores: float32 [1024], P(('center', 'expert'))
The draws below stay inside these ranges and needn't reach their ends.
Inputs may be any that keep to these rules, and one draw needn't show every extreme that they name: `expert_ids`: each row names 8 different experts; in the rows of one device no expert is named by more than 16 rows, a bound that some block reaches. `doc_ids`: each row splits its 128 tokens into 8 runs numbered in order, each of 1 to 32 tokens, one of exactly 32.
All inputs are finite; a program needn't handle non-finite values.
Results may differ from the reference program's by a relative error of at most 0.0071.
Values may be sent and summed in bfloat16 or wider, within the bound.
A program may use at most 128 MiB of HBM per device.

```python
import math
import jax
import jax.numpy as jnp
import numpy as np
from jax import lax

D = 2048
FF = 768
TOP = 8
TOK_DEV = 128
DOC_MOST = 32
SHARDS = 128
EXPERTS = 128
CAP = 16
DOC_DEV = 8
TOKENS = 16384
DOCS = 1024
CENTERS = 32768


def shared_features(key):
    chosen_count = min(16, D // 4)
    feature_order = jax.random.permutation(jax.random.fold_in(key, 9173), D)
    strong = (feature_order < chosen_count).astype(jnp.float32)
    return (strong, chosen_count)


def draw_down(key, part):
    strong, chosen_count = shared_features(key)
    own_key = jax.random.fold_in(key, 311)
    values = jnp.clip(jax.random.normal(own_key, (EXPERTS, FF, D), jnp.float32), -4.0, 4.0)
    column_scale = (0.5 + 5.5 * strong) / math.sqrt(FF)
    return (values * column_scale[None, None, :]).astype(jnp.bfloat16)


def draw_bank(key, part):
    strong, chosen_count = shared_features(key)
    direction_key = jax.random.fold_in(key, 401)
    rough_key = jax.random.fold_in(key, 402)
    radius_key = jax.random.fold_in(key, 403)
    direction = jnp.clip(jax.random.normal(direction_key, (CENTERS, D), jnp.float32), -4.0, 4.0)
    rough = jnp.clip(jax.random.normal(rough_key, (CENTERS, D), jnp.float32), -4.0, 4.0)
    radius = jnp.exp(jax.random.uniform(radius_key, (CENTERS,), jnp.float32, math.log(0.35), math.log(1.0)))
    planted = radius[:, None] * direction * strong[None, :] / math.sqrt(chosen_count)
    background = 0.3 * rough * (1.0 - strong[None, :]) / math.sqrt(D)
    return (planted + background).astype(jnp.bfloat16)


def level_of(stream_key, dims, pieces, least, high):
    gain = 1.0
    for axis_at, parts in pieces:
        heights = jax.random.uniform(jax.random.fold_in(jax.random.fold_in(stream_key, 6), axis_at), (parts,), jnp.float32, least / len(pieces), high / len(pieces))
        gain = gain * jnp.repeat(jnp.exp(heights), dims[axis_at] // parts).reshape((-1,) + (1,) * (len(dims) - 1 - axis_at))
    return gain


def profile(amount, total, most, slope):
    portions = [(1 << 20) // math.isqrt(standing ** slope) + 1 for standing in range(2, amount + 1)]
    surplus, counts = total - most - (amount - 1), [1] * (amount - 1)
    while surplus > 0:
        candidates = [i for i in range(amount - 1) if counts[i] < most]
        pool, remaining = sum([portions[i] for i in candidates]), surplus
        for i in candidates:
            extra = min(most - counts[i], max(1, remaining * portions[i] // pool), surplus)
            counts[i] = counts[i] + extra
            surplus = surplus - extra
    return np.array([most] + counts)


def ragged(key, number_of, total, bound, slope):
    if number_of == 2:
        one = jax.random.randint(key, (), max(1, total - bound), min(bound, total - 1) + 1)
        return jnp.stack([one, total - one])
    lengths = jnp.asarray(profile(number_of, total, bound, slope), jnp.int32)
    pairs = (number_of - 1) // 2
    donor, taker = lengths[1:1 + 2 * pairs:2], lengths[2:2 + 2 * pairs:2]
    room = jnp.minimum(donor - 1, bound - taker)
    moved = jax.random.randint(jax.random.fold_in(key, 1), (pairs,), 0, 1 << 20) % (room + 1)
    lengths = lengths.at[1:1 + 2 * pairs:2].set(donor - moved).at[2:2 + 2 * pairs:2].set(taker + moved)
    return lengths[jax.random.permutation(jax.random.fold_in(key, 2), number_of)]


def assign_block(key, own, number, rows, amount, top, most, lean):
    sequence = jax.random.permutation(key, amount)
    crowded, common = load_shares(amount, rows * top, most, lean, True), load_shares(amount, rows * top, most, lean, False)
    places = jnp.arange(amount)

    def named(lengths, rotation):
        used = int((lengths > 0).sum())
        fixed = max(1, used // 4)
        moved = fixed + (places - fixed + rotation * (used - fixed)) % max(1, amount - fixed)
        return jnp.zeros((amount,), jnp.int32).at[sequence[jnp.where(places < fixed, places, moved)]].set(jnp.asarray(lengths, jnp.int32))

    lengths = jnp.where(number % 4 == 0, named(crowded, number // 4), named(common, number - number // 4 - 1))
    mixed = jax.random.permutation(jax.random.fold_in(own, 3), amount)
    source_of, sink = mixed[0:amount // 2 * 2:2], mixed[1:amount // 2 * 2:2]
    room = jnp.minimum(lengths[source_of] - 1, most - lengths[sink]) // 2
    room = jnp.where((source_of == sequence[0]) | (sink == sequence[0]) | (lengths[sink] == 0), 0, jnp.maximum(room, 0))
    moved = jax.random.randint(jax.random.fold_in(own, 4), (amount // 2,), 0, 1 << 20) % (room + 1)
    lengths = lengths.at[source_of].add(-moved).at[sink].add(moved)
    members = jnp.searchsorted(jnp.cumsum(lengths), jnp.arange(rows * top), side="right").astype(jnp.int32)
    listing = members.reshape(top, rows).T
    listing = listing[jax.random.permutation(jax.random.fold_in(own, 1), rows)]
    rotation = jax.random.randint(jax.random.fold_in(own, 2), (rows, 1), 0, top)
    return jnp.take_along_axis(listing, (jnp.arange(top)[None, :] + rotation) % top, axis=1)


def load_shares(number_of, total, limit, lean, full):
    portions = [(1 << 20) // math.isqrt(standing ** lean) + 1 for standing in range(1, number_of + 1)]
    largest = limit if full else min(limit, max(-(-total // number_of), total * portions[0] // sum(portions)))
    least = 1 if total - largest >= number_of - 1 else 0
    counts, spare = [largest] + [least] * (number_of - 1), total - largest - least * (number_of - 1)
    while spare > 0:
        candidates = [i for i in range(1, number_of) if counts[i] < largest] or [i for i in range(1, number_of) if counts[i] < limit]
        mass, remaining = sum([portions[i] for i in candidates]), spare
        for i in candidates:
            addition = min(limit - counts[i], max(1, remaining * portions[i] // mass), spare)
            counts[i] = counts[i] + addition
            spare = spare - addition
    return np.array(counts)


def scatter_about(stream_key, shape, deviation, limit, shards=(), kind=jnp.bfloat16):
    result = jax.random.normal(stream_key, shape, jnp.float32) * deviation
    if len(shards) > 0:
        result = level_of(stream_key, shape, shards, -0.22, 0.18) * result
    return jnp.clip(result, min=-limit, max=limit).astype(kind)


def setup_inputs(seed: int = 0) -> dict:
    arg_keys = jax.random.split(jax.random.key(seed), 8)
    tokens = scatter_about(arg_keys[0], (TOKENS, D), 1.0, 6.0, ((0, 128),))
    doc_ids = jax.vmap(lambda own: jnp.searchsorted(jnp.cumsum(ragged(own, DOC_DEV, TOK_DEV, DOC_MOST, 1)), jnp.arange(TOK_DEV), side="right"))(jax.random.split(arg_keys[1], SHARDS)).reshape((SHARDS, TOK_DEV)).astype(jnp.int32)
    expert_ids_keys = jax.random.split(jax.random.fold_in(arg_keys[2], 1), TOKENS // TOK_DEV)
    expert_ids_turns = jax.random.permutation(jax.random.fold_in(arg_keys[2], 3), TOKENS // TOK_DEV)
    expert_ids = jax.vmap(lambda own, number: assign_block(jax.random.fold_in(arg_keys[2], 2), own, number, TOK_DEV, EXPERTS, TOP, CAP, 1))(expert_ids_keys, expert_ids_turns).reshape((TOKENS, TOP))
    gate_raw = jnp.clip(jnp.exp(math.log(1.0) - 2.3025851 * jax.random.uniform(arg_keys[3], (TOKENS, TOP), jnp.float32) ** level_of(arg_keys[3], (TOKENS, TOP), ((0, 128),), -0.2, 0.2)), 0.1, 1.0)
    gate_up = scatter_about(arg_keys[4], (EXPERTS, D, 2 * FF), D ** -0.5, 0.125, ((0, 128),))
    down = draw_down(jax.random.fold_in(arg_keys[7], 71), 0)
    bank = draw_bank(jax.random.fold_in(arg_keys[7], 71), 0)
    return {"tokens": tokens, "doc_ids": doc_ids, "expert_ids": expert_ids, "gate_raw": gate_raw, "gate_up": gate_up, "down": down, "bank": bank}


def rms_normed(hidden_rows):
    values = hidden_rows.astype(jnp.float32)
    inverse_rms = lax.rsqrt(lax.optimization_barrier(jnp.mean(values * values, axis=-1, keepdims=True)) + 1e-06)
    return (values * inverse_rms).astype(jnp.bfloat16)

def slot_table(chosen_ids, expert_count):
    chosen = (chosen_ids[:, :, None] == jnp.arange(expert_count, dtype=jnp.int32)[None, None, :]).astype(jnp.int32)
    per_token = lax.optimization_barrier(jnp.sum(chosen, axis=1))
    before = jnp.cumsum(per_token, axis=0) - per_token
    return lax.optimization_barrier(jnp.sum(chosen * before[:, None, :], axis=2)).astype(jnp.int32)

def expert_ffn(rows_in, weights_gu, weights_down):
    hidden_width = weights_down.shape[0]
    gate_and_up = jnp.dot(rows_in, weights_gu, preferred_element_type=jnp.float32)
    hidden = (jax.nn.silu(gate_and_up[:, :hidden_width]) * gate_and_up[:, hidden_width:]).astype(jnp.bfloat16)
    return jnp.dot(hidden, weights_down, preferred_element_type=jnp.float32).astype(jnp.bfloat16)

def reference(tokens, doc_ids, expert_ids, gate_raw, gate_up, down, bank):
    normed = rms_normed(tokens)
    ids_shard = expert_ids.reshape(SHARDS, TOK_DEV, TOP)
    position = jax.vmap(lambda chosen_ids: slot_table(chosen_ids, EXPERTS))(ids_shard)
    shard_of = jnp.broadcast_to(jnp.arange(SHARDS, dtype=jnp.int32)[:, None, None], ids_shard.shape)
    token_of = jnp.broadcast_to(jnp.arange(TOKENS, dtype=jnp.int32).reshape(SHARDS, TOK_DEV)[:, :, None], ids_shard.shape)
    row_table = jnp.full((EXPERTS, SHARDS, CAP), TOKENS, jnp.int32).at[ids_shard, shard_of, position].set(token_of)
    padded = jnp.concatenate([normed, jnp.zeros((1, D), jnp.bfloat16)], axis=0)

    def one_expert(expert_index):
        picked_rows = padded[row_table[expert_index].reshape(-1)]
        return expert_ffn(picked_rows, gate_up[expert_index], down[expert_index])
    outputs = lax.map(one_expert, jnp.arange(EXPERTS, dtype=jnp.int32)).reshape(EXPERTS, SHARDS, CAP, D)
    gate_norm = gate_raw / lax.optimization_barrier(jnp.sum(gate_raw, axis=1, keepdims=True))
    gate_shard = gate_norm.reshape(SHARDS, TOK_DEV, TOP)

    def combine_shard(shard_index):
        picked = outputs[ids_shard[shard_index], shard_index, position[shard_index]]
        return lax.optimization_barrier(jnp.sum(picked.astype(jnp.float32) * gate_shard[shard_index][:, :, None], axis=1))
    combined = lax.map(combine_shard, jnp.arange(SHARDS, dtype=jnp.int32))
    layer_out = combined.reshape(TOKENS, D).astype(jnp.bfloat16)
    member = (jnp.arange(DOC_DEV, dtype=jnp.int32)[None, :, None] == doc_ids[:, None, :]).astype(jnp.float32)
    summed = jnp.einsum('sjt,std->sjd', member, combined, precision=lax.Precision.HIGHEST)
    summed = summed.reshape(DOCS, D)
    pooled = (summed * lax.rsqrt(lax.optimization_barrier(jnp.sum(summed * summed, axis=1, keepdims=True)) + 1e-06)).astype(jnp.bfloat16)
    bank_values = bank.astype(jnp.float32)
    bank_norms = lax.optimization_barrier(jnp.sum(bank_values * bank_values, axis=1))

    def score_shard(doc_block):
        doc_values = doc_block.astype(jnp.float32)
        doc_norms = lax.optimization_barrier(jnp.sum(doc_values * doc_values, axis=1))
        products = jnp.dot(doc_block, bank.T, preferred_element_type=jnp.float32)
        distance = doc_norms[:, None] + bank_norms[None, :] - 2.0 * products
        return lax.optimization_barrier(jnp.min(distance, axis=1))
    scores = lax.map(score_shard, pooled.reshape(SHARDS, DOC_DEV, D)).reshape(DOCS)
    return (layer_out, scores)
```

```python
import functools

import jax
import jax.numpy as jnp
from jax import lax
from jax.experimental import pallas as pl
from jax.experimental.pallas import tpu as pltpu
from jax.sharding import PartitionSpec as P

MESH = pl.DeviceIdType.MESH
D = 2048
FF = 768
TOK = 128
CAP = 16
DOC_DEV = 8
COLS = ((0, 768), (768, 640), (1408, 640))
ORDER = ((0, 1, 2), (1, 2, 0), (2, 0, 1))
BF = jnp.bfloat16
F32 = jnp.float32


def where_am_i():
    center = lax.axis_index("center")
    expert = lax.axis_index("expert")
    return (lax.rem(center, 4), lax.div(center, 4), lax.div(expert, 2)), lax.rem(expert, 2)


def wrap(v):
    return lax.rem(v + 4, 4)


def device_at(xyz, core):
    return (xyz[1] * 4 + xyz[0], xyz[2] * 2 + core)


def moved(xyz, axis, delta):
    out = list(xyz)
    out[axis] = wrap(out[axis] + delta)
    return tuple(out)


def enter(peers):
    barrier = pltpu.get_barrier_semaphore()
    for peer in peers:
        pl.semaphore_signal(barrier, 1, device_id=peer, device_id_type=MESH)
    return lambda: pl.semaphore_wait(barrier, len(peers))


def line_peers(xyz, core):
    peers = [device_at(xyz, 1 - core)]
    for axis in range(3):
        for delta in (1, 2, 3):
            for other in (core, 1 - core):
                peers.append(device_at(moved(xyz, axis, delta), other))
    return peers


def remote(src, dst, send, recv, dev):
    return pltpu.make_async_remote_copy(
        src_ref=src, dst_ref=dst, send_sem=send, recv_sem=recv, device_id=dev, device_id_type=MESH
    )


def rows_of(ref, g, b, c, core):
    if g == 0:
        return ref.at[b, :, c, core]
    if g == 1:
        return ref.at[:, c, b, core]
    return ref.at[c, b, :, core]


def expert_number(g, xyz, core_of, c):
    at = list(xyz)
    at[ORDER[g][2]] = c
    return (at[1] * 4 + at[0]) * 8 + at[2] * 2 + core_of


R_TO_DELTA = (0, 1, 3, 2)
BREL = (0, 3, 1, 2)


def dispatch_kernel(
    tok_ref, meta_ref, tri_ref, x0, x1, x2, qg_ref,
    g0, g1, g2, s0, s1, s2, m_ref,
    p1s, p1r, p2s, p2r, fs, fr, m1s, m1r, m2s, m2r, ps, pr, loc,
):
    xyz, core = where_am_i()
    outs, held, sent = (x0, x1, x2), (g0, g1, g2), (s0, s1, s2)
    ready = enter(line_peers(xyz, core))

    for q in range(4):
        rows = pl.ds(q * 32, 32)
        values = tok_ref[rows, :].astype(F32)
        scale = lax.rsqrt(jnp.mean(values * values, axis=-1, keepdims=True) + 1e-06)
        normed = (values * scale).astype(BF)
        for g in range(3):
            a, b = xyz[ORDER[g][0]], xyz[ORDER[g][1]]
            held[g][b, a, rows, :] = normed[:, COLS[g][0]:COLS[g][0] + COLS[g][1]]
    for g in range(3):
        a, b = xyz[ORDER[g][0]], xyz[ORDER[g][1]]
        m_ref[g, b, a] = meta_ref[...]
    ready()

    def along(g, which, delta):
        return device_at(moved(xyz, ORDER[g][which], delta), core)

    def meta1(g, d):
        a, b = xyz[ORDER[g][0]], xyz[ORDER[g][1]]
        blk = m_ref.at[g, b, a]
        return remote(blk, blk, m1s.at[g, d - 1], m1r.at[g, d - 1], along(g, 0, d))

    def meta2(g, d):
        b = xyz[ORDER[g][1]]
        blk = m_ref.at[g, b]
        return remote(blk, blk, m2s.at[g, d - 1], m2r.at[g, d - 1], along(g, 1, d))

    def first(g, d):
        a, b = xyz[ORDER[g][0]], xyz[ORDER[g][1]]
        blk = held[g].at[b, a]
        return remote(blk, blk, p1s.at[g, d - 1], p1r.at[g, d - 1], along(g, 0, d))

    def second(g, direction, r):
        a, b = xyz[ORDER[g][0]], xyz[ORDER[g][1]]
        blk = held[g].at[b, wrap(a - R_TO_DELTA[r])]
        return remote(
            blk, blk, p2s.at[g, direction, r], p2r.at[g, direction, r],
            along(g, 1, 1 if direction == 0 else 3),
        )

    def onward(g, r):
        a, b = xyz[ORDER[g][0]], xyz[ORDER[g][1]]
        direction = r % 2
        blk = held[g].at[wrap(b + (3 if direction == 0 else 1)), wrap(a - R_TO_DELTA[r])]
        return remote(
            blk, blk, fs.at[g, r], fr.at[g, r], along(g, 1, 1 if direction == 0 else 3)
        )

    for g in range(3):
        for d in (1, 3, 2):
            meta1(g, d).start()
    for g in range(3):
        for d in (1, 3, 2):
            first(g, d).start()
    for g in range(3):
        for direction in range(2):
            second(g, direction, 0).start()
    for g in range(3):
        for d in (1, 3, 2):
            meta1(g, d).wait_recv()
        for d in (1, 3, 2):
            meta2(g, d).start()
    for r in (1, 2, 3):
        for g in range(3):
            first(g, R_TO_DELTA[r]).wait_recv()
            for direction in range(2):
                second(g, direction, r).start()

    def select(g, brel):
        a_axis, b_axis, c_axis = ORDER[g]
        b = wrap(xyz[b_axis] + brel)
        ids = m_ref[g, b, :, 0:8, :]
        gates = m_ref[g, b, :, 8:16, :]
        sub = lax.broadcasted_iota(jnp.int32, (4, 8, TOK), 1)
        named = jnp.zeros((4, 8, TOK), F32)
        gated = jnp.zeros((4, 8, TOK), F32)
        for j in range(8):
            number = expert_number(g, xyz, j % 2, j // 2).astype(F32)
            hit = ids == number
            named = jnp.where(sub == j, jnp.sum(jnp.where(hit, 1.0, 0.0), axis=1, keepdims=True), named)
            gated = jnp.where(sub == j, jnp.sum(jnp.where(hit, gates, 0.0), axis=1, keepdims=True), gated)
        before = jnp.dot(
            named.reshape(32, TOK).astype(BF), tri_ref[...], preferred_element_type=F32
        ).reshape(4, 8, TOK)
        qg_ref[g, b, :, 0:8, :] = jnp.where(named > 0.5, before, -1.0)
        qg_ref[g, b, :, 8:16, :] = gated
        slot = lax.broadcasted_iota(jnp.int32, (8, CAP, TOK), 1).astype(F32)

        def body(a, carry):
            place = qg_ref[g, b, a, 0:8, :]
            pick = jnp.where(place[:, None, :] == slot, 1.0, 0.0).reshape(8 * CAP, TOK).astype(BF)
            rows = jnp.dot(pick, held[g][b, a], preferred_element_type=F32).astype(BF)
            sent[g][brel, :, a] = rows.reshape(8, CAP, COLS[g][1])
            return carry

        lax.fori_loop(0, 4, body, 0)

    def third(g, brel, dc, dk):
        c_axis = ORDER[g][2]
        c, b = xyz[c_axis], wrap(xyz[ORDER[g][1]] + brel)
        target, other = wrap(c + dc), (core if dk == 0 else 1 - core)
        src = sent[g].at[brel, target * 2 + other]
        dst = rows_of(outs[g], g, b, c, core)
        if dc == 0 and dk == 0:
            return pltpu.make_async_copy(src, dst, loc.at[g, brel])
        return remote(src, dst, ps.at[g], pr.at[g], device_at(moved(xyz, c_axis, dc), other))

    def send_rows(g, brel):
        for dc in (2, 1, 3, 0):
            for dk in (0, 1):
                third(g, brel, dc, dk).start()

    for g in range(3):
        select(g, 0)
        send_rows(g, 0)
    for r in range(4):
        for g in range(3):
            second(g, r % 2, r).wait_recv()
            onward(g, r).start()
    for g in range(3):
        for d in (1, 3, 2):
            meta2(g, d).wait_recv()
    for direction, brel in ((0, 3), (1, 1)):
        for g in range(3):
            for r in range(4):
                if r % 2 != direction:
                    second(g, direction, r).wait_recv()
            select(g, brel)
            send_rows(g, brel)
    for g in range(3):
        for r in range(4):
            onward(g, r).wait_recv()
        select(g, 2)
        send_rows(g, 2)
    for g in range(3):
        for d in (1, 2, 3):
            meta1(g, d).wait_send()
            meta2(g, d).wait_send()
            first(g, d).wait_send()
        for r in range(4):
            onward(g, r).wait_send()
            for direction in range(2):
                second(g, direction, r).wait_send()
        for brel in range(4):
            third(g, brel, 0, 0).wait()
        whole = remote(
            sent[g].at[:, 0:7], sent[g].at[:, 0:7], ps.at[g], pr.at[g], device_at(xyz, 1 - core)
        )
        whole.wait_send()
        whole.wait_recv()


def dispatch(tokens, meta, tri):
    any_spec, vmem = pl.BlockSpec(memory_space=pl.ANY), pl.BlockSpec(memory_space=pltpu.VMEM)
    dma = pltpu.SemaphoreType.DMA
    return pl.pallas_call(
        dispatch_kernel,
        out_shape=[jax.ShapeDtypeStruct((4, 4, 4, 2, CAP, w), BF) for _, w in COLS]
        + [jax.ShapeDtypeStruct((3, 4, 4, 16, TOK), F32)],
        in_specs=[vmem] * 3,
        out_specs=[any_spec] * 3 + [vmem],
        scratch_shapes=[pltpu.VMEM((4, 4, TOK, w), BF) for _, w in COLS]
        + [pltpu.VMEM((4, 8, 4, CAP, w), BF) for _, w in COLS]
        + [pltpu.VMEM((3, 4, 4, 16, TOK), F32)]
        + [dma((3, 3)), dma((3, 3)), dma((3, 2, 4)), dma((3, 2, 4)), dma((3, 4)), dma((3, 4))]
        + [dma((3, 3))] * 4
        + [dma((3,)), dma((3,)), dma((3, 4))],
        compiler_params=pltpu.CompilerParams(
            collective_id=0, has_side_effects=True, vmem_limit_bytes=40 << 20
        ),
        name="dispatch",
    )(tokens, meta, tri)


def ffn_kernel(x0, x1, x2, wgu, wd, y0, y1, y2):
    total = None
    for ref, (at, width) in zip((x0, x1, x2), COLS):
        part = jnp.dot(ref[...], wgu[at:at + width, :], preferred_element_type=F32)
        total = part if total is None else total + part
    gate, up = total[:, :FF], total[:, FF:]
    hidden = (gate / (1.0 + jnp.exp(-gate)) * up).astype(BF)
    for ref, (at, width) in zip((y0, y1, y2), COLS):
        ref[...] = jnp.dot(hidden, wd[:, at:at + width], preferred_element_type=F32).astype(BF)


def ffn(xs, wgu, wd):
    rows, step = 2048, 256
    flat = [x.reshape(rows, -1) for x in xs]
    blocks = [pl.BlockSpec((step, w), lambda i: (i, 0)) for _, w in COLS]
    outs = pl.pallas_call(
        ffn_kernel,
        grid=(rows // step,),
        out_shape=[jax.ShapeDtypeStruct((rows, w), BF) for _, w in COLS],
        in_specs=blocks
        + [
            pl.BlockSpec((D, 2 * FF), lambda i: (0, 0), pipeline_mode=pl.Buffered(1)),
            pl.BlockSpec((FF, D), lambda i: (0, 0), pipeline_mode=pl.Buffered(1)),
        ],
        out_specs=blocks,
        compiler_params=pltpu.CompilerParams(vmem_limit_bytes=48 << 20),
        name="ffn",
    )(*flat, wgu, wd)
    return [y.reshape(4, 4, 4, 2, CAP, -1) for y in outs]


def combine_kernel(
    y0, y1, y2, qg_ref, doc_ref, out_ref, pooled_ref,
    r30, r31, r32, h0, h1, h2, r20, r21, r22, r10, r11, r12, comb,
    c3s, c3r, loc, c2s, c2r, c1s, c1r,
):
    xyz, core = where_am_i()
    ys, back, part = (y0, y1, y2), (r30, r31, r32), (h0, h1, h2)
    sums, last = (r20, r21, r22), (r10, r11, r12)
    enter(line_peers(xyz, core))()

    def third(g, brel, dc, dk):
        c_axis = ORDER[g][2]
        c, b = xyz[c_axis], wrap(xyz[ORDER[g][1]] + brel)
        target, other = wrap(c + dc), (core if dk == 0 else 1 - core)
        src = rows_of(ys[g], g, b, target, other)
        dst = back[g].at[b, :, c * 2 + core]
        if dc == 0 and dk == 0:
            return pltpu.make_async_copy(src, dst, loc.at[g, brel])
        return remote(
            src, dst, c3s.at[g, brel], c3r.at[g, brel], device_at(moved(xyz, c_axis, dc), other)
        )

    def third_all(g, brel):
        b = wrap(xyz[ORDER[g][1]] + brel)
        blk = back[g].at[b, :, 0:7]
        return remote(blk, blk, c3s.at[g, brel], c3r.at[g, brel], device_at(xyz, 1 - core))

    def second(g, brel):
        b_axis = ORDER[g][1]
        b = wrap(xyz[b_axis] + brel)
        return remote(
            part[g].at[b], sums[g].at[brel - 1], c2s.at[g, brel - 1], c2r.at[g, brel - 1],
            device_at(moved(xyz, b_axis, brel), core),
        )

    def first(g, arel):
        a_axis, b_axis, _ = ORDER[g]
        a, b = wrap(xyz[a_axis] + arel), xyz[b_axis]
        return remote(
            part[g].at[b, a], last[g].at[arel - 1], c1s.at[g, arel - 1], c1r.at[g, arel - 1],
            device_at(moved(xyz, a_axis, arel), core),
        )

    for brel in (2, 1, 3, 0):
        for g in range(3):
            for dc in (2, 1, 3, 0):
                for dk in (0, 1):
                    third(g, brel, dc, dk).start()

    slot = lax.broadcasted_iota(jnp.int32, (8, CAP, TOK), 1).astype(F32)
    contract = (((0,), (0,)), ((), ()))
    for brel in (2, 1, 3, 0):
        for g in range(3):
            b = wrap(xyz[ORDER[g][1]] + brel)
            third(g, brel, 0, 0).wait()
            third_all(g, brel).wait_recv()

            def body(a, carry, g=g, b=b):
                place, gates = qg_ref[g, b, a, 0:8, :], qg_ref[g, b, a, 8:16, :]
                weight = jnp.where(place[:, None, :] == slot, gates[:, None, :], 0.0)
                weight = weight.reshape(8 * CAP, TOK)
                high = weight.astype(BF)
                low = (weight - high.astype(F32)).astype(BF)
                rows = back[g][b, a].reshape(8 * CAP, COLS[g][1])
                total = lax.dot_general(high, rows, contract, preferred_element_type=F32)
                total += lax.dot_general(low, rows, contract, preferred_element_type=F32)
                part[g][b, a] = total.astype(BF)
                return carry

            lax.fori_loop(0, 4, body, 0)
            if brel:
                second(g, brel).start()
    for g in range(3):
        a_axis, b_axis, _ = ORDER[g]
        b = xyz[b_axis]
        for brel in (1, 2, 3):
            second(g, brel).wait_recv()
        for arel in (2, 1, 3, 0):
            a = wrap(xyz[a_axis] + arel)
            total = part[g][b, a].astype(F32)
            for i in range(3):
                total += sums[g][i, a].astype(F32)
            if arel:
                part[g][b, a] = total.astype(BF)
                first(g, arel).start()
            else:
                comb[:, COLS[g][0]:COLS[g][0] + COLS[g][1]] = total
    for g in range(3):
        for arel in (1, 2, 3):
            first(g, arel).wait_recv()
        at, width = COLS[g]
        total = comb[:, at:at + width]
        for i in range(3):
            total += last[g][i].astype(F32)
        comb[:, at:at + width] = total
        out_ref[:, at:at + width] = total.astype(BF)
    doc = lax.broadcasted_iota(jnp.int32, (DOC_DEV, TOK), 0)
    member = jnp.where(doc == doc_ref[...], 1.0, 0.0)
    summed = jnp.dot(
        member, comb[...], precision=lax.Precision.HIGHEST, preferred_element_type=F32
    )
    pooled_ref[...] = (
        summed * lax.rsqrt(jnp.sum(summed * summed, axis=1, keepdims=True) + 1e-06)
    ).astype(BF)
    for g in range(3):
        for brel in range(4):
            third_all(g, brel).wait_send()
        for d in (1, 2, 3):
            second(g, d).wait_send()
            first(g, d).wait_send()


def combine(ys, qg, doc_ids):
    any_spec, vmem = pl.BlockSpec(memory_space=pl.ANY), pl.BlockSpec(memory_space=pltpu.VMEM)
    dma = pltpu.SemaphoreType.DMA
    return pl.pallas_call(
        combine_kernel,
        out_shape=[
            jax.ShapeDtypeStruct((TOK, D), BF),
            jax.ShapeDtypeStruct((DOC_DEV, D), BF),
        ],
        in_specs=[any_spec] * 3 + [vmem] * 2,
        out_specs=[vmem] * 2,
        scratch_shapes=[pltpu.VMEM((4, 4, 8, CAP, w), BF) for _, w in COLS]
        + [pltpu.VMEM((4, 4, TOK, w), BF) for _, w in COLS]
        + [pltpu.VMEM((3, 4, TOK, w), BF) for _, w in COLS]
        + [pltpu.VMEM((3, TOK, w), BF) for _, w in COLS]
        + [pltpu.VMEM((TOK, D), F32)]
        + [dma((3, 4))] * 3
        + [dma((3, 3))] * 4,
        compiler_params=pltpu.CompilerParams(
            collective_id=1, has_side_effects=True, vmem_limit_bytes=48 << 20
        ),
        name="combine",
    )(*ys, qg, doc_ids)


def score_kernel(pooled_ref, bank_ref, out_ref, docs, best, near, gs, gr, ns, nr):
    center, expert = lax.axis_index("center"), lax.axis_index("expert")
    others = [(lax.rem(center + d, 16), expert) for d in range(1, 16)]
    ready = enter(others)
    docs[center] = pooled_ref[...]
    ready()

    def gather(d):
        return remote(docs.at[center], docs.at[center], gs.at[d - 1], gr.at[d - 1], others[d - 1])

    def tell(d):
        return remote(best, near.at[center], ns.at[d - 1], nr.at[d - 1], others[d - 1])

    for d in range(1, 16):
        gather(d).start()
    for d in range(1, 16):
        gather(d).wait_recv()
    block = docs[...].reshape(16 * DOC_DEV, D)
    values = block.astype(F32)
    nearest = jnp.full((1, 128), jnp.inf, F32)

    def body(i, nearest):
        rows = bank_ref[pl.ds(pl.multiple_of(i * 256, 256), 256), :]
        wide = rows.astype(F32)
        norms = jnp.sum(wide * wide, axis=1, keepdims=True)
        products = lax.dot_general(
            rows, block, (((1,), (1,)), ((), ())), preferred_element_type=F32
        )
        return jnp.minimum(nearest, jnp.min(norms - 2.0 * products, axis=0, keepdims=True))

    nearest = lax.fori_loop(0, 8, body, nearest)
    best[...] = jnp.broadcast_to(nearest, (8, 128))
    near[center] = jnp.broadcast_to(nearest, (8, 128))
    for d in range(1, 16):
        tell(d).start()
    ones = jnp.ones((8, D), F32)
    doc_norms = lax.dot_general(
        ones, values * values, (((1,), (1,)), ((), ())),
        precision=lax.Precision.HIGHEST, preferred_element_type=F32,
    )
    for d in range(1, 16):
        tell(d).wait_recv()
    out_ref[...] = jnp.min(near[...], axis=0) + doc_norms
    for d in range(1, 16):
        gather(d).wait_send()
        tell(d).wait_send()


def score(pooled, bank):
    vmem = pl.BlockSpec(memory_space=pltpu.VMEM)
    dma = pltpu.SemaphoreType.DMA
    return pl.pallas_call(
        score_kernel,
        out_shape=jax.ShapeDtypeStruct((8, 128), F32),
        in_specs=[vmem] * 2,
        out_specs=vmem,
        scratch_shapes=[
            pltpu.VMEM((16, DOC_DEV, D), BF),
            pltpu.VMEM((8, 128), F32),
            pltpu.VMEM((16, 8, 128), F32),
        ]
        + [dma((15,))] * 4,
        compiler_params=pltpu.CompilerParams(
            collective_id=2, has_side_effects=True, vmem_limit_bytes=40 << 20
        ),
        name="score",
    )(pooled, bank)


def local(tokens, doc_ids, expert_ids, gate_raw, gate_up, down, bank):
    gates = gate_raw.T
    gates = gates / jnp.sum(gates, axis=0, keepdims=True)
    meta = jnp.concatenate([expert_ids.T.astype(F32), gates], axis=0)
    tri = jnp.triu(jnp.ones((TOK, TOK), F32), 1).astype(BF)
    *xs, qg = dispatch(tokens, meta, tri)
    ys = ffn(xs, gate_up[0], down[0])
    layer_out, pooled = combine(ys, qg, doc_ids)
    scores = score(pooled, bank)
    own = lax.dynamic_slice_in_dim(scores[0], lax.axis_index("center") * DOC_DEV, DOC_DEV)
    return layer_out, own


def solution(mesh):
    return jax.shard_map(
        local,
        mesh=mesh,
        in_specs=(
            P(("center", "expert"), None),
            P(("center", "expert"), None),
            P(("center", "expert"), None),
            P(("center", "expert"), None),
            P(("center", "expert"), None, None),
            P(("center", "expert"), None, None),
            P("center", None),
        ),
        out_specs=(P(("center", "expert"), None), P(("center", "expert"))),
        check_vma=False,
    )
```

```python
import functools

import jax
import jax.numpy as jnp
from jax import lax
from jax.experimental import pallas as pl
from jax.experimental.pallas import tpu as pltpu
from jax.sharding import PartitionSpec as P

MESH = pl.DeviceIdType.MESH
D = 2048
FF = 768
TOK = 128
CAP = 16
DOC_DEV = 8
COLS = ((0, 768), (768, 640), (1408, 640))
ORDER = ((0, 1, 2), (1, 2, 0), (2, 0, 1))
BF = jnp.bfloat16
F32 = jnp.float32


def where_am_i():
    center = lax.axis_index("center")
    expert = lax.axis_index("expert")
    return (lax.rem(center, 4), lax.div(center, 4), lax.div(expert, 2)), lax.rem(expert, 2)


def wrap(v):
    return lax.rem(v + 4, 4)


def device_at(xyz, core):
    return (xyz[1] * 4 + xyz[0], xyz[2] * 2 + core)


def moved(xyz, axis, delta):
    out = list(xyz)
    out[axis] = wrap(out[axis] + delta)
    return tuple(out)


def enter(peers):
    barrier = pltpu.get_barrier_semaphore()
    for peer in peers:
        pl.semaphore_signal(barrier, 1, device_id=peer, device_id_type=MESH)
    return lambda: pl.semaphore_wait(barrier, len(peers))


def line_peers(xyz, core):
    peers = [device_at(xyz, 1 - core)]
    for axis in range(3):
        for delta in (1, 2, 3):
            for other in (core, 1 - core):
                peers.append(device_at(moved(xyz, axis, delta), other))
    return peers


def remote(src, dst, send, recv, dev):
    return pltpu.make_async_remote_copy(
        src_ref=src, dst_ref=dst, send_sem=send, recv_sem=recv, device_id=dev, device_id_type=MESH
    )


def rows_of(ref, g, b, c, core):
    if g == 0:
        return ref.at[b, :, c, core]
    if g == 1:
        return ref.at[:, c, b, core]
    return ref.at[c, b, :, core]


def expert_number(g, xyz, core_of, c):
    at = list(xyz)
    at[ORDER[g][2]] = c
    return (at[1] * 4 + at[0]) * 8 + at[2] * 2 + core_of


R_TO_DELTA = (0, 1, 3, 2)
BREL = (0, 3, 1, 2)

OFF = (2, 1, 3, 0)


def layer_kernel(
    tok_ref, ids_ref, gate_ref, doc_ref, wgu_hbm, wd_hbm, bank_hbm,
    out_ref, score_ref, x0, x1, x2,
    m_ref, qg_ref, tri_ref, cw_ref, h0, h1, h2, s0, s1, s2,
    wgu, wd, xb, r30, r31, r32, f0, f1, f2, r20, r21, r22, r10, r11, r12,
    comb, docs, best, near, norms,
    p1s, p1r, p2s, p2r, fs, fr, m1s, m1r, m2s, m2r, ps, pr, loc1,
    wsem, xsem, bsem, c3s, c3r, loc, hs, hr, c2s, c2r, c1s, c1r, gs, gr, ns, nr,
):
    xyz, core = where_am_i()
    x, y, z = xyz
    center = lax.axis_index("center")
    outs, back, held, sent = (x0, x1, x2), (r30, r31, r32), (h0, h1, h2), (s0, s1, s2)
    part = held
    halves, sums, last = (f0, f1, f2), (r20, r21, r22), (r10, r11, r12)
    spans = [pl.ds(at, width) for at, width in COLS]
    plane = [(dx, dy) for dy in range(4) for dx in range(4) if dx or dy]
    mates = [device_at((wrap(x + dx), wrap(y + dy), z), core) for dx, dy in plane]
    ready = enter(
        line_peers(xyz, core) + [m for m, (dx, dy) in zip(mates, plane) if dx and dy]
    )
    load_w = [
        pltpu.make_async_copy(wgu_hbm, wgu, wsem.at[0]),
        pltpu.make_async_copy(wd_hbm, wd, wsem.at[1]),
    ]
    for q in range(4):
        rows = pl.ds(q * 32, 32)
        values = tok_ref[rows, :].astype(F32)
        scale = lax.rsqrt(jnp.mean(values * values, axis=-1, keepdims=True) + 1e-06)
        normed = (values * scale).astype(BF)
        for g in range(3):
            a, b = xyz[ORDER[g][0]], xyz[ORDER[g][1]]
            held[g][b, a, rows, :] = normed[:, COLS[g][0]:COLS[g][0] + COLS[g][1]]
    gates = gate_ref[...]
    gates = gates / jnp.sum(gates, axis=0, keepdims=True)
    ids = ids_ref[...].astype(F32)
    for g in range(3):
        a, b = xyz[ORDER[g][0]], xyz[ORDER[g][1]]
        m_ref[g, b, a, 0:8, :] = ids
        m_ref[g, b, a, 8:16, :] = gates
    earlier = lax.broadcasted_iota(jnp.int32, (TOK, TOK), 0)
    later = lax.broadcasted_iota(jnp.int32, (TOK, TOK), 1)
    tri_ref[...] = jnp.where(earlier < later, 1.0, 0.0).astype(BF)
    ready()
    for copy in load_w:
        copy.start()

    def along(g, which, delta):
        return device_at(moved(xyz, ORDER[g][which], delta), core)

    def meta1(g, d):
        a, b = xyz[ORDER[g][0]], xyz[ORDER[g][1]]
        blk = m_ref.at[g, b, a]
        return remote(blk, blk, m1s.at[g, d - 1], m1r.at[g, d - 1], along(g, 0, d))

    def meta2(g, d):
        b = xyz[ORDER[g][1]]
        blk = m_ref.at[g, b]
        return remote(blk, blk, m2s.at[g, d - 1], m2r.at[g, d - 1], along(g, 1, d))

    def spread1(g, d):
        a, b = xyz[ORDER[g][0]], xyz[ORDER[g][1]]
        blk = held[g].at[b, a]
        return remote(blk, blk, p1s.at[g, d - 1], p1r.at[g, d - 1], along(g, 0, d))

    def spread2(g, direction, r):
        a, b = xyz[ORDER[g][0]], xyz[ORDER[g][1]]
        blk = held[g].at[b, wrap(a - R_TO_DELTA[r])]
        return remote(
            blk, blk, p2s.at[g, direction, r], p2r.at[g, direction, r],
            along(g, 1, 1 if direction == 0 else 3),
        )

    def onward(g, r):
        a, b = xyz[ORDER[g][0]], xyz[ORDER[g][1]]
        direction = r % 2
        blk = held[g].at[wrap(b + (3 if direction == 0 else 1)), wrap(a - R_TO_DELTA[r])]
        return remote(
            blk, blk, fs.at[g, r], fr.at[g, r], along(g, 1, 1 if direction == 0 else 3)
        )

    for g in range(3):
        for d in (1, 3, 2):
            meta1(g, d).start()
    for g in range(3):
        for d in (1, 3, 2):
            spread1(g, d).start()
    for g in range(3):
        for direction in range(2):
            spread2(g, direction, 0).start()
    for g in range(3):
        for d in (1, 3, 2):
            meta1(g, d).wait_recv()
        for d in (1, 3, 2):
            meta2(g, d).start()
    for r in (1, 2, 3):
        for g in range(3):
            spread1(g, R_TO_DELTA[r]).wait_recv()
            for direction in range(2):
                spread2(g, direction, r).start()

    def select(g, brel):
        a_axis, b_axis, c_axis = ORDER[g]
        b = wrap(xyz[b_axis] + brel)
        ids = m_ref[g, b, :, 0:8, :]
        gates = m_ref[g, b, :, 8:16, :]
        sub = lax.broadcasted_iota(jnp.int32, (4, 8, TOK), 1)
        named = jnp.zeros((4, 8, TOK), F32)
        gated = jnp.zeros((4, 8, TOK), F32)
        for j in range(8):
            number = expert_number(g, xyz, j % 2, j // 2).astype(F32)
            hit = ids == number
            named = jnp.where(sub == j, jnp.sum(jnp.where(hit, 1.0, 0.0), axis=1, keepdims=True), named)
            gated = jnp.where(sub == j, jnp.sum(jnp.where(hit, gates, 0.0), axis=1, keepdims=True), gated)
        before = jnp.dot(
            named.reshape(32, TOK).astype(BF), tri_ref[...], preferred_element_type=F32
        ).reshape(4, 8, TOK)
        qg_ref[g, b, :, 0:8, :] = jnp.where(named > 0.5, before, -1.0)
        qg_ref[g, b, :, 8:16, :] = gated
        slot = lax.broadcasted_iota(jnp.int32, (8, CAP, TOK), 1).astype(F32)

        def body(a, carry):
            place = qg_ref[g, b, a, 0:8, :]
            pick = jnp.where(place[:, None, :] == slot, 1.0, 0.0).reshape(8 * CAP, TOK).astype(BF)
            rows = jnp.dot(pick, held[g][b, a], preferred_element_type=F32).astype(BF)
            sent[g][brel, a] = rows.reshape(4, 2, CAP, COLS[g][1])
            return carry

        lax.fori_loop(0, 4, body, 0)

    def rows_out(g, brel, dc, dk):
        c_axis = ORDER[g][2]
        c, b = xyz[c_axis], wrap(xyz[ORDER[g][1]] + brel)
        target, other = wrap(c + dc), (core if dk == 0 else 1 - core)
        src = sent[g].at[brel, :, target, other]
        dst = rows_of(outs[g], g, b, c, core)
        if dc == 0 and dk == 0:
            return pltpu.make_async_copy(src, dst, loc1.at[g, brel])
        return remote(src, dst, ps.at[g], pr.at[g], device_at(moved(xyz, c_axis, dc), other))

    def send_rows(g, brel):
        for dc in (2, 1, 3, 0):
            for dk in (0, 1):
                rows_out(g, brel, dc, dk).start()

    for g in range(3):
        select(g, 0)
        send_rows(g, 0)
    for r in range(4):
        for g in range(3):
            spread2(g, r % 2, r).wait_recv()
            onward(g, r).start()
    for g in range(3):
        for d in (1, 3, 2):
            meta2(g, d).wait_recv()
    for direction, brel in ((0, 3), (1, 1)):
        for g in range(3):
            for r in range(4):
                if r % 2 != direction:
                    spread2(g, direction, r).wait_recv()
            select(g, brel)
            send_rows(g, brel)
    for g in range(3):
        for r in range(4):
            onward(g, r).wait_recv()
        select(g, 2)
        send_rows(g, 2)
    def weigh(i, carry):
        b, a = lax.div(i, 4), lax.rem(i, 4)
        for g in range(3):
            place, gate = qg_ref[g, b, a, 0:8, :], qg_ref[g, b, a, 8:16, :]
            slots = lax.broadcasted_iota(jnp.int32, (8, CAP, TOK), 1).astype(F32)
            weight = jnp.where(place[:, None, :] == slots, gate[:, None, :], 0.0)
            weight = weight.reshape(8 * CAP, TOK).T
            high = weight.astype(BF)
            cw_ref[g, b, a, :, 0:TOK] = high
            cw_ref[g, b, a, :, TOK:2 * TOK] = (weight - high.astype(F32)).astype(BF)
        return carry

    lax.fori_loop(0, 16, weigh, 0)
    for g in range(3):
        for d in (1, 2, 3):
            meta1(g, d).wait_send()
            meta2(g, d).wait_send()
            spread1(g, d).wait_send()
        for r in range(4):
            onward(g, r).wait_send()
            for direction in range(2):
                spread2(g, direction, r).wait_send()
        for brel in range(4):
            rows_out(g, brel, 0, 0).wait()
        whole = remote(
            back[g].at[:, :, 0:7], back[g].at[:, :, 0:7], ps.at[g], pr.at[g],
            device_at(xyz, 1 - core),
        )
        whole.wait_send()
        whole.wait_recv()

    def load_x(s):
        row = wrap(y + OFF[s])
        return [
            pltpu.make_async_copy(
                outs[g].at[row], xb.at[s % 2, :, :, :, :, spans[g]], xsem.at[s % 2, g]
            )
            for g in range(3)
        ]

    load_bank = [
        pltpu.make_async_copy(bank_hbm.at[:, :, :, :, spans[g]], back[g], bsem.at[g])
        for g in range(3)
    ]
    for copy in load_x(0):
        copy.start()

    def third(g, s, part_x, dc, dk):
        row = wrap(y + OFF[s])
        other = core if dk == 0 else 1 - core
        axis = ORDER[g][2]
        mine = xyz[axis] * 2 + core
        self_copy = type(dc) is int and dc == 0 and dk == 0
        target = wrap(xyz[axis] + dc)
        if g == 0:
            src, dst = sent[0].at[row, part_x, target, other], back[0].at[row, part_x, mine]
        elif g == 1:
            src, dst = sent[1].at[row, target, :, other], back[1].at[:, row, mine]
        else:
            src, dst = sent[2].at[row, part_x, :, other], back[2].at[part_x, :, mine]
        if self_copy:
            return pltpu.make_async_copy(src, dst, loc.at[g, s])
        return remote(
            src, dst, c3s.at[g, s], c3r.at[g, s], device_at(moved(xyz, axis, dc), other)
        )

    def third_all(g, s):
        row = wrap(y + OFF[s])
        if g == 0:
            blk = back[0].at[row, :, 0:7]
        elif g == 1:
            blk = back[1].at[:, row, 0:7]
        else:
            blk = back[2].at[:, :, 0:(2 if s < 3 else 1)]
        return remote(blk, blk, c3s.at[g, s], c3r.at[g, s], device_at(xyz, 1 - core))

    def half(g, direction):
        a0 = 2 * direction
        return remote(
            part[g].at[wrap(xyz[ORDER[g][1]] + 2), a0:a0 + 2], halves[g].at[direction],
            hs.at[g, direction], hr.at[g, direction],
            device_at(moved(xyz, ORDER[g][1], 1 if direction == 0 else 3), core),
        )

    def second(g, direction):
        step = 1 if direction == 0 else 3
        return remote(
            part[g].at[wrap(xyz[ORDER[g][1]] + step)], sums[g].at[direction],
            c2s.at[g, direction], c2r.at[g, direction],
            device_at(moved(xyz, ORDER[g][1], step), core),
        )

    def first(g, arel):
        a_axis, b_axis, _ = ORDER[g]
        return remote(
            part[g].at[xyz[b_axis], wrap(xyz[a_axis] + arel)], last[g].at[arel - 1],
            c1s.at[g, arel - 1], c1r.at[g, arel - 1],
            device_at(moved(xyz, a_axis, arel), core),
        )

    def total_of(g, b, a):
        rows = back[g][b, a].reshape(8 * CAP, COLS[g][1])
        return jnp.dot(
            cw_ref[g, b, a], jnp.concatenate([rows, rows], axis=0), preferred_element_type=F32
        )

    def combine(g, brel):
        b = wrap(xyz[ORDER[g][1]] + brel)

        def plain(a, carry):
            part[g][b, a] = total_of(g, b, a).astype(BF)
            return carry

        if brel in (0, 2):
            lax.fori_loop(0, 4, plain, 0)
            if brel == 2:
                half(g, 0).start()
                half(g, 1).start()
            return
        direction = 0 if brel == 1 else 1
        a0 = 2 * direction
        lax.fori_loop(2 - a0, 4 - a0, plain, 0)
        half(g, direction).wait_recv()

        def added(a, carry):
            total = total_of(g, b, a) + halves[g][direction, a - a0].astype(F32)
            part[g][b, a] = total.astype(BF)
            return carry

        lax.fori_loop(a0, a0 + 2, added, 0)
        second(g, direction).start()

    def received(g, s):
        if g == 0:
            for part_x in x_parts:
                third(0, s, part_x, 0, 0).wait()
        elif g == 1:
            third(1, s, None, 0, 0).wait()
        elif s == 3:
            for part_x in x_parts:
                third(2, s, part_x, 0, 0).wait()
        third_all(g, s).wait_recv()

    own_half = lax.div(x, 2)
    x_parts = (pl.ds(2 * (1 - own_half), 2), pl.ds(2 * own_half, 2))
    for s in range(4):
        for copy in load_x(s):
            copy.wait()
        if s < 3:
            for copy in load_x(s + 1):
                copy.start()
        if s == 0:
            for copy in load_w:
                copy.wait()
        row = wrap(y + OFF[s])
        for h in range(2):
            part_x = x_parts[h]
            rows = xb[s % 2, part_x].reshape(256, D)
            both = jnp.dot(rows, wgu[...], preferred_element_type=F32)
            gate, up = both[:, :FF], both[:, FF:]
            hidden = (gate / (1.0 + jnp.exp(-gate)) * up).astype(BF)
            result = jnp.dot(hidden, wd[...], preferred_element_type=F32).astype(BF)
            for g in range(3):
                at, width = COLS[g]
                sent[g][row, part_x] = result[:, at:at + width].reshape(2, 4, 2, CAP, width)
            for dc in (2, 1, 3, 0):
                for dk in (0, 1):
                    third(0, s, part_x, dc, dk).start()
            for dk in (0, 1):
                third(2, s, part_x, OFF[s], dk).start()
            if h == 0:
                dcs = [2 * (1 - own_half) - x, 2 * (1 - own_half) + 1 - x]
            else:
                dcs = [1 - 2 * lax.rem(x, 2), 0]
            for dc in dcs:
                for dk in (0, 1):
                    third(1, s, None, dc, dk).start()
        if s == 2:
            received(0, 0)
            combine(0, 2)
    for s in range(4):
        for g in (1, 2):
            received(g, s)
    combine(1, 2)
    combine(2, 2)
    received(0, 1)
    combine(0, 1)
    combine(1, 1)
    combine(2, 1)
    received(0, 2)
    combine(0, 3)
    combine(1, 3)
    combine(2, 3)
    received(0, 3)
    for g in range(3):
        combine(g, 0)
    for copy in load_bank:
        copy.start()
    for copy in load_bank:
        copy.wait()

    def norm(i, carry):
        total = jnp.zeros((128, 1), F32)
        for g in range(3):
            wide = back[g][lax.div(i, 4), lax.rem(i, 4)].reshape(128, COLS[g][1]).astype(F32)
            total += jnp.sum(wide * wide, axis=1, keepdims=True)
        norms[i] = jnp.broadcast_to(total, (128, 128))
        return carry

    lax.fori_loop(0, 16, norm, 0)

    for g in range(3):
        a_axis, b_axis, _ = ORDER[g]
        b = xyz[b_axis]
        second(g, 0).wait_recv()
        second(g, 1).wait_recv()
        for arel in (2, 1, 3, 0):
            a = wrap(xyz[a_axis] + arel)
            total = part[g][b, a].astype(F32)
            for i in range(2):
                total += sums[g][i, a].astype(F32)
            if arel:
                part[g][b, a] = total.astype(BF)
                first(g, arel).start()
            else:
                comb[:, spans[g]] = total
    for g in range(3):
        for arel in (1, 2, 3):
            first(g, arel).wait_recv()
        total = comb[:, spans[g]]
        for i in range(3):
            total += last[g][i].astype(F32)
        comb[:, spans[g]] = total
        out_ref[:, spans[g]] = total.astype(BF)
    doc = lax.broadcasted_iota(jnp.int32, (DOC_DEV, TOK), 0)
    member = jnp.where(doc == doc_ref[...], 1.0, 0.0)
    summed = jnp.dot(
        member, comb[...], precision=lax.Precision.HIGHEST, preferred_element_type=F32
    )
    pooled = (
        summed * lax.rsqrt(jnp.sum(summed * summed, axis=1, keepdims=True) + 1e-06)
    ).astype(BF)
    docs[center] = pooled

    def gather(i):
        return remote(docs.at[center], docs.at[center], gs.at[i], gr.at[i], mates[i])

    def tell(i):
        return remote(best, near.at[center], ns.at[i], nr.at[i], mates[i])

    for i in range(15):
        gather(i).start()
    wide = pooled.astype(F32)
    own = jnp.sum(wide * wide, axis=1, keepdims=True)
    lane = lax.broadcasted_iota(jnp.int32, (DOC_DEV, 128), 1)
    sub = lax.broadcasted_iota(jnp.int32, (DOC_DEV, 128), 0)
    own = jnp.sum(jnp.where(lane == center * DOC_DEV + sub, own, 0.0), axis=0, keepdims=True)
    for i in range(15):
        gather(i).wait_recv()
    block = docs[...].reshape(16 * DOC_DEV, D)

    def nearest_of(i, nearest):
        products = jnp.zeros((512, 128), F32)
        for g in range(3):
            at, width = COLS[g]
            products += lax.dot_general(
                back[g][i].reshape(512, width), block[:, at:at + width],
                (((1,), (1,)), ((), ())), preferred_element_type=F32,
            )
        distance = norms[pl.ds(i * 4, 4)].reshape(512, 128) - 2.0 * products
        return jnp.minimum(nearest, jnp.min(distance.reshape(64, 8, 128), axis=0))

    nearest = lax.fori_loop(0, 4, nearest_of, jnp.full((8, 128), jnp.inf, F32))
    best[...] = nearest
    near[center] = nearest
    for i in range(15):
        tell(i).start()
    for i in range(15):
        tell(i).wait_recv()
    closest = jnp.min(jnp.min(near[...], axis=0), axis=0, keepdims=True)
    mine = pltpu.roll(closest + own, lax.rem(128 - center * DOC_DEV, 128), 1)
    score_ref[...] = mine[:, 0:DOC_DEV]
    for g in range(3):
        for s in range(4):
            third_all(g, s).wait_send()
        for direction in range(2):
            half(g, direction).wait_send()
            second(g, direction).wait_send()
        for d in (1, 2, 3):
            first(g, d).wait_send()
    for i in range(15):
        gather(i).wait_send()
        tell(i).wait_send()


def layer(tokens, ids, gates, doc_ids, wgu, wd, bank):
    any_spec, vmem = pl.BlockSpec(memory_space=pl.ANY), pl.BlockSpec(memory_space=pltpu.VMEM)
    dma = pltpu.SemaphoreType.DMA
    return pl.pallas_call(
        layer_kernel,
        out_shape=[
            jax.ShapeDtypeStruct((TOK, D), BF),
            jax.ShapeDtypeStruct((1, DOC_DEV), F32),
        ]
        + [jax.ShapeDtypeStruct((4, 4, 4, 2, CAP, w), BF) for _, w in COLS],
        in_specs=[vmem] * 4 + [any_spec] * 3,
        out_specs=[vmem] * 2 + [any_spec] * 3,
        scratch_shapes=[
            pltpu.VMEM((3, 4, 4, 16, TOK), F32),
            pltpu.VMEM((3, 4, 4, 16, TOK), F32),
            pltpu.VMEM((TOK, TOK), BF),
            pltpu.VMEM((3, 4, 4, TOK, 2 * TOK), BF),
        ]
        + [pltpu.VMEM((4, 4, TOK, w), BF) for _, w in COLS]
        + [pltpu.VMEM((4, 4, 4, 2, CAP, w), BF) for _, w in COLS]
        + [
            pltpu.VMEM((D, 2 * FF), BF),
            pltpu.VMEM((FF, D), BF),
            pltpu.VMEM((2, 4, 4, 2, CAP, D), BF),
        ]
        + [pltpu.VMEM((4, 4, 8, CAP, w), BF) for _, w in COLS]
        + [pltpu.VMEM((2, 2, TOK, w), BF) for _, w in COLS]
        + [pltpu.VMEM((2, 4, TOK, w), BF) for _, w in COLS]
        + [pltpu.VMEM((3, TOK, w), BF) for _, w in COLS]
        + [
            pltpu.VMEM((TOK, D), F32),
            pltpu.VMEM((16, DOC_DEV, D), BF),
            pltpu.VMEM((8, 128), F32),
            pltpu.VMEM((16, 8, 128), F32),
            pltpu.VMEM((16, 128, 128), F32),
        ]
        + [dma((3, 3)), dma((3, 3)), dma((3, 2, 4)), dma((3, 2, 4)), dma((3, 4)), dma((3, 4))]
        + [dma((3, 3))] * 4
        + [dma((3,)), dma((3,)), dma((3, 4))]
        + [dma((2,)), dma((2, 3)), dma((3,))]
        + [dma((3, 4))] * 3
        + [dma((3, 2))] * 4
        + [dma((3, 3))] * 2
        + [dma((15,))] * 4,
        compiler_params=pltpu.CompilerParams(
            collective_id=0, has_side_effects=True, vmem_limit_bytes=63 << 20
        ),
        name="layer",
    )(tokens, ids, gates, doc_ids, wgu, wd, bank)


def local(tokens, doc_ids, expert_ids, gate_raw, gate_up, down, bank):
    layer_out, scores, *_ = layer(
        tokens, expert_ids.T, gate_raw.T, doc_ids, gate_up[0], down[0],
        bank.reshape(4, 4, 8, CAP, D),
    )
    return layer_out, scores.reshape(DOC_DEV)


def solution(mesh):
    return jax.shard_map(
        local,
        mesh=mesh,
        in_specs=(
            P(("center", "expert"), None),
            P(("center", "expert"), None),
            P(("center", "expert"), None),
            P(("center", "expert"), None),
            P(("center", "expert"), None, None),
            P(("center", "expert"), None, None),
            P("center", None),
        ),
        out_specs=(P(("center", "expert"), None), P(("center", "expert"))),
        check_vma=False,
    )
```

```python
import functools

import jax
import jax.numpy as jnp
from jax import lax
from jax.experimental import pallas as pl
from jax.experimental.pallas import tpu as pltpu
from jax.sharding import PartitionSpec as P

MESH = pl.DeviceIdType.MESH
D = 2048
FF = 768
TOK = 128
CAP = 16
DOC_DEV = 8
COLS = ((0, 768), (768, 640), (1408, 640))
ORDER = ((0, 1, 2), (1, 2, 0), (2, 0, 1))
BF = jnp.bfloat16
F32 = jnp.float32


def where_am_i():
    center = lax.axis_index("center")
    expert = lax.axis_index("expert")
    return (lax.rem(center, 4), lax.div(center, 4), lax.div(expert, 2)), lax.rem(expert, 2)


def wrap(v):
    return lax.rem(v + 4, 4)


def turned(xyz, k):
    x, y, z = xyz
    return (x + k * (y - x), y + k * (z - y), z + k * (x - z))


def straight(uvw, k):
    u, v, w = uvw
    return (u + k * (w - u), v + k * (u - v), w + k * (v - w))


def real_device(xyz, core):
    return (xyz[1] * 4 + xyz[0], xyz[2] * 2 + core)


def device_at(uvw, k, core):
    return real_device(straight(uvw, k), core)


def moved(uvw, axis, delta):
    out = list(uvw)
    out[axis] = wrap(out[axis] + delta)
    return tuple(out)


def enter(peers):
    barrier = pltpu.get_barrier_semaphore()
    for peer in peers:
        pl.semaphore_signal(barrier, 1, device_id=peer, device_id_type=MESH)
    return lambda: pl.semaphore_wait(barrier, len(peers))


def line_peers(xyz, core):
    peers = [real_device(xyz, 1 - core)]
    for axis in range(3):
        for delta in (1, 2, 3):
            for other in (core, 1 - core):
                peers.append(real_device(moved(xyz, axis, delta), other))
    return peers


def remote(src, dst, send, recv, dev):
    return pltpu.make_async_remote_copy(
        src_ref=src, dst_ref=dst, send_sem=send, recv_sem=recv, device_id=dev, device_id_type=MESH
    )


def rows_of(ref, g, b, c, core):
    cols = pl.ds(*COLS[g])
    if g == 0:
        return ref.at[core, b, :, c, :, cols]
    if g == 1:
        return ref.at[core, :, c, b, :, cols]
    return ref.at[core, c, b, :, :, cols]


def expert_number(g, uvw, core, k, c):
    at = list(uvw)
    at[ORDER[g][2]] = c
    x, y, z = straight(at, core)
    return (y * 4 + x) * 8 + z * 2 + k


R_TO_DELTA = (0, 1, 3, 2)
BREL = (0, 3, 1, 2)

OFF = (2, 1, 3, 0)


def layer_kernel(
    tok_ref, ids_ref, gate_ref, doc_ref, wgu_hbm, wd_hbm, bank_hbm,
    out_ref, score_ref,
    m_ref, qg_ref, tri_ref, cw_ref, h0, h1, h2, s0, s1, s2,
    wgu, wd, xv, r30, r31, r32, f0, f1, f2, r20, r21, r22, r10, r11, r12,
    comb, docs, best, near, norms, q0, q1, q2, q20, q21, q22, q10, q11, q12, summed,
    p1s, p1r, p2s, p2r, fs, fr, m1s, m1r, m2s, m2r, ps, pr, loc1,
    wsem, bsem, c3s, c3r, loc, hs, hr, c2s, c2r, c1s, c1r, d2s, d2r, d1s, d1r, gs, gr, ns, nr,
):
    xyz, core = where_am_i()
    x, y, z = xyz
    uvw = turned(xyz, core)
    center = lax.axis_index("center")
    back, held, sent = (r30, r31, r32), (h0, h1, h2), (s0, s1, s2)
    part = held
    halves, sums, last = (f0, f1, f2), (r20, r21, r22), (r10, r11, r12)
    pools, pools2, pools1 = (q0, q1, q2), (q20, q21, q22), (q10, q11, q12)
    spans = [pl.ds(at, width) for at, width in COLS]
    plane = [(dx, dy) for dy in range(4) for dx in range(4) if dx or dy]
    mates = [real_device((wrap(x + dx), wrap(y + dy), z), core) for dx, dy in plane]
    ready = enter(
        line_peers(xyz, core) + [m for m, (dx, dy) in zip(mates, plane) if dx and dy]
    )
    load_w = [
        pltpu.make_async_copy(wgu_hbm, wgu, wsem.at[0]),
        pltpu.make_async_copy(wd_hbm, wd, wsem.at[1]),
    ]
    for q in range(4):
        rows = pl.ds(q * 32, 32)
        values = tok_ref[rows, :].astype(F32)
        scale = lax.rsqrt(jnp.mean(values * values, axis=-1, keepdims=True) + 1e-06)
        normed = (values * scale).astype(BF)
        for g in range(3):
            a, b = uvw[ORDER[g][0]], uvw[ORDER[g][1]]
            held[g][b, a, rows, :] = normed[:, COLS[g][0]:COLS[g][0] + COLS[g][1]]
    gates = gate_ref[...]
    gates = gates / jnp.sum(gates, axis=0, keepdims=True)
    ids = ids_ref[...].astype(F32)
    for g in range(3):
        a, b = uvw[ORDER[g][0]], uvw[ORDER[g][1]]
        m_ref[g, b, a, 0:8, :] = ids
        m_ref[g, b, a, 8:16, :] = gates
        m_ref[g, b, a, 16:24, :] = jnp.broadcast_to(doc_ref[...].astype(F32), (8, TOK))
    earlier = lax.broadcasted_iota(jnp.int32, (TOK, TOK), 0)
    later = lax.broadcasted_iota(jnp.int32, (TOK, TOK), 1)
    tri_ref[...] = jnp.where(earlier < later, 1.0, 0.0).astype(BF)
    ready()
    for copy in load_w:
        copy.start()

    def along(g, which, delta):
        return device_at(moved(uvw, ORDER[g][which], delta), core, core)

    def meta1(g, d):
        a, b = uvw[ORDER[g][0]], uvw[ORDER[g][1]]
        blk = m_ref.at[g, b, a]
        return remote(blk, blk, m1s.at[g, d - 1], m1r.at[g, d - 1], along(g, 0, d))

    def meta2(g, d):
        b = uvw[ORDER[g][1]]
        blk = m_ref.at[g, b]
        return remote(blk, blk, m2s.at[g, d - 1], m2r.at[g, d - 1], along(g, 1, d))

    def spread1(g, d):
        a, b = uvw[ORDER[g][0]], uvw[ORDER[g][1]]
        blk = held[g].at[b, a]
        return remote(blk, blk, p1s.at[g, d - 1], p1r.at[g, d - 1], along(g, 0, d))

    def spread2(g, direction, r):
        a, b = uvw[ORDER[g][0]], uvw[ORDER[g][1]]
        blk = held[g].at[b, wrap(a - R_TO_DELTA[r])]
        return remote(
            blk, blk, p2s.at[g, direction, r], p2r.at[g, direction, r],
            along(g, 1, 1 if direction == 0 else 3),
        )

    def onward(g, r):
        a, b = uvw[ORDER[g][0]], uvw[ORDER[g][1]]
        direction = r % 2
        blk = held[g].at[wrap(b + (3 if direction == 0 else 1)), wrap(a - R_TO_DELTA[r])]
        return remote(
            blk, blk, fs.at[g, r], fr.at[g, r], along(g, 1, 1 if direction == 0 else 3)
        )

    for g in range(3):
        for d in (1, 3, 2):
            meta1(g, d).start()
    for g in range(3):
        for d in (1, 3, 2):
            spread1(g, d).start()
    for g in range(3):
        for direction in range(2):
            spread2(g, direction, 0).start()
    for g in range(3):
        for d in (1, 3, 2):
            meta1(g, d).wait_recv()
        for d in (1, 3, 2):
            meta2(g, d).start()
    for r in (1, 2, 3):
        for g in range(3):
            spread1(g, R_TO_DELTA[r]).wait_recv()
            for direction in range(2):
                spread2(g, direction, r).start()

    def select(g, brel):
        a_axis, b_axis, c_axis = ORDER[g]
        b = wrap(uvw[b_axis] + brel)
        ids = m_ref[g, b, :, 0:8, :]
        gates = m_ref[g, b, :, 8:16, :]
        sub = lax.broadcasted_iota(jnp.int32, (4, 8, TOK), 1)
        named = jnp.zeros((4, 8, TOK), F32)
        gated = jnp.zeros((4, 8, TOK), F32)
        for j in range(8):
            number = expert_number(g, uvw, core, j // 4, j % 4).astype(F32)
            hit = ids == number
            named = jnp.where(sub == j, jnp.sum(jnp.where(hit, 1.0, 0.0), axis=1, keepdims=True), named)
            gated = jnp.where(sub == j, jnp.sum(jnp.where(hit, gates, 0.0), axis=1, keepdims=True), gated)
        before = jnp.dot(
            named.reshape(32, TOK).astype(BF), tri_ref[...], preferred_element_type=F32
        ).reshape(4, 8, TOK)
        qg_ref[g, b, :, 0:8, :] = jnp.where(named > 0.5, before, -1.0)
        qg_ref[g, b, :, 8:16, :] = gated
        slot = lax.broadcasted_iota(jnp.int32, (8, CAP, TOK), 1).astype(F32)

        def body(a, carry):
            place = qg_ref[g, b, a, 0:8, :]
            pick = jnp.where(place[:, None, :] == slot, 1.0, 0.0).reshape(8 * CAP, TOK).astype(BF)
            rows = jnp.dot(pick, held[g][b, a], preferred_element_type=F32).astype(BF)
            sent[g][:, brel, a] = rows.reshape(2, 4, CAP, COLS[g][1])
            return carry

        lax.fori_loop(0, 4, body, 0)

    def rows_out(g, brel, dc, dk):
        c_axis = ORDER[g][2]
        c, b = uvw[c_axis], wrap(uvw[ORDER[g][1]] + brel)
        target, other = wrap(c + dc), (core if dk == 0 else 1 - core)
        src = sent[g].at[other, brel, :, target]
        dst = rows_of(xv, g, b, c, core)
        if dc == 0 and dk == 0:
            return pltpu.make_async_copy(src, dst, loc1.at[g, brel])
        return remote(src, dst, ps.at[g], pr.at[g], device_at(moved(uvw, c_axis, dc), core, other))

    def send_rows(g, brel):
        for dc in (2, 1, 3, 0):
            for dk in (0, 1):
                rows_out(g, brel, dc, dk).start()

    for g in range(3):
        select(g, 0)
        send_rows(g, 0)
    for r in range(4):
        for g in range(3):
            spread2(g, r % 2, r).wait_recv()
            onward(g, r).start()
    for g in range(3):
        for d in (1, 3, 2):
            meta2(g, d).wait_recv()
    for direction, brel in ((0, 3), (1, 1)):
        for g in range(3):
            for r in range(4):
                if r % 2 != direction:
                    spread2(g, direction, r).wait_recv()
            select(g, brel)
            send_rows(g, brel)
    for g in range(3):
        for r in range(4):
            onward(g, r).wait_recv()
        select(g, 2)
        send_rows(g, 2)
    def weigh(i, carry):
        b, a = lax.div(i, 4), lax.rem(i, 4)
        for g in range(3):
            place, gate = qg_ref[g, b, a, 0:8, :], qg_ref[g, b, a, 8:16, :]
            slots = lax.broadcasted_iota(jnp.int32, (8, CAP, TOK), 1).astype(F32)
            weight = jnp.where(place[:, None, :] == slots, gate[:, None, :], 0.0)
            weight = weight.reshape(8 * CAP, TOK).T
            high = weight.astype(BF)
            low = (weight - high.astype(F32)).astype(BF)
            cw_ref[g, b, a, 0:TOK, 0:TOK] = high
            cw_ref[g, b, a, 0:TOK, TOK:2 * TOK] = low
            number = lax.broadcasted_iota(jnp.int32, (16, TOK), 0).astype(F32)
            member = jnp.where(m_ref[g, b, a, 16:17, :] == number, 1.0, 0.0).astype(BF)
            pool = jnp.dot(member, high, preferred_element_type=F32)
            pool += jnp.dot(member, low, preferred_element_type=F32)
            high = pool.astype(BF)
            cw_ref[g, b, a, TOK:TOK + 16, 0:TOK] = high
            cw_ref[g, b, a, TOK:TOK + 16, TOK:2 * TOK] = (pool - high.astype(F32)).astype(BF)
        return carry

    lax.fori_loop(0, 16, weigh, 0)
    for g in range(3):
        for d in (1, 2, 3):
            meta1(g, d).wait_send()
            meta2(g, d).wait_send()
            spread1(g, d).wait_send()
        for r in range(4):
            onward(g, r).wait_send()
            for direction in range(2):
                spread2(g, direction, r).wait_send()
        for brel in range(4):
            rows_out(g, brel, 0, 0).wait()
        whole = remote(
            back[g].at[:, :, 0:7], back[g].at[:, :, 0:7], ps.at[g], pr.at[g],
            real_device(xyz, 1 - core),
        )
        whole.wait_send()
        whole.wait_recv()

    load_bank = [
        pltpu.make_async_copy(bank_hbm.at[:, :, :, :, spans[g]], back[g], bsem.at[g])
        for g in range(3)
    ]

    def third(g, s, h, dc, dk):
        other = core if dk == 0 else 1 - core
        at = turned(xyz, other)
        axis = ORDER[g][2]
        row, part_u = wrap(at[1] + OFF[s]), u_parts(at[0])[h]
        mine = core * 4 + at[axis]
        target = wrap(at[axis] + dc)
        if g == 0:
            src, dst = sent[0].at[other, row, part_u, target], back[0].at[row, part_u, mine]
        elif g == 1:
            src, dst = sent[1].at[other, row, target], back[1].at[:, row, mine]
        else:
            src, dst = sent[2].at[other, row, part_u], back[2].at[part_u, :, mine]
        if type(dc) is int and dc == 0 and dk == 0:
            return pltpu.make_async_copy(src, dst, loc.at[g, s])
        return remote(
            src, dst, c3s.at[g, s], c3r.at[g, s], device_at(moved(at, axis, dc), other, other)
        )

    def u_parts(u):
        own_half = lax.div(u, 2)
        return (pl.ds(2 * (1 - own_half), 2), pl.ds(2 * own_half, 2))

    def third_all(g, s):
        row = wrap(uvw[1] + OFF[s])
        if g == 0:
            blk = back[0].at[row, :, 0:7]
        elif g == 1:
            blk = back[1].at[:, row, 0:7]
        else:
            blk = back[2].at[:, :, 0:(2 if s < 3 else 1)]
        return remote(blk, blk, c3s.at[g, s], c3r.at[g, s], real_device(xyz, 1 - core))

    def half(g, direction):
        a0 = 2 * direction
        return remote(
            part[g].at[wrap(uvw[ORDER[g][1]] + 2), a0:a0 + 2], halves[g].at[direction],
            hs.at[g, direction], hr.at[g, direction],
            device_at(moved(uvw, ORDER[g][1], 1 if direction == 0 else 3), core, core),
        )

    def second(g, direction, a):
        step = 1 if direction == 0 else 3
        return remote(
            part[g].at[wrap(uvw[ORDER[g][1]] + step), a], sums[g].at[direction, a],
            c2s.at[g, direction, a], c2r.at[g, direction, a],
            device_at(moved(uvw, ORDER[g][1], step), core, core),
        )

    def first(g, arel):
        a_axis, b_axis, _ = ORDER[g]
        return remote(
            part[g].at[uvw[b_axis], wrap(uvw[a_axis] + arel)], last[g].at[arel - 1],
            c1s.at[g, arel - 1], c1r.at[g, arel - 1],
            device_at(moved(uvw, a_axis, arel), core, core),
        )

    def total_of(g, b, a):
        rows = back[g][b, a].reshape(8 * CAP, COLS[g][1])
        total = jnp.dot(
            cw_ref[g, b, a], jnp.concatenate([rows, rows], axis=0), preferred_element_type=F32
        )
        pools[g][b, a] = total[TOK:TOK + DOC_DEV].astype(BF)
        return total[0:TOK]

    def pool_second(g, brel):
        b_axis = ORDER[g][1]
        return remote(
            pools[g].at[wrap(uvw[b_axis] + brel)], pools2[g].at[brel - 1],
            d2s.at[g, brel - 1], d2r.at[g, brel - 1],
            device_at(moved(uvw, b_axis, brel), core, core),
        )

    def pool_first(g, arel):
        a_axis, b_axis, _ = ORDER[g]
        return remote(
            pools[g].at[uvw[b_axis], wrap(uvw[a_axis] + arel)], pools1[g].at[arel - 1],
            d1s.at[g, arel - 1], d1r.at[g, arel - 1],
            device_at(moved(uvw, a_axis, arel), core, core),
        )

    def combine(g, brel):
        b = wrap(uvw[ORDER[g][1]] + brel)

        def plain(a, carry):
            part[g][b, a] = total_of(g, b, a).astype(BF)
            return carry

        lax.fori_loop(0, 4, plain, 0)
        if brel == 2:
            half(g, 0).start()
            half(g, 1).start()

    def combine_near(g, direction):
        b = wrap(uvw[ORDER[g][1]] + (1 if direction == 0 else 3))

        def plain(a, carry):
            part[g][b, a] = total_of(g, b, a).astype(BF)
            second(g, direction, a).start()
            return carry

        a0 = 2 - 2 * direction
        lax.fori_loop(a0, a0 + 2, plain, 0)

    def combine_on(g, direction, i):
        b = wrap(uvw[ORDER[g][1]] + (1 if direction == 0 else 3))
        a = 2 * direction + i
        total = total_of(g, b, a) + halves[g][direction, i].astype(F32)
        part[g][b, a] = total.astype(BF)
        second(g, direction, a).start()

    def received(g, s):
        if g == 0:
            for h in range(2):
                third(0, s, h, 0, 0).wait()
        elif g == 1:
            third(1, s, 1, 0, 0).wait()
        elif s == 3:
            for h in range(2):
                third(2, s, h, 0, 0).wait()
        third_all(g, s).wait_recv()

    for s in range(4):
        if s == 0:
            for copy in load_w:
                copy.wait()
        for h in range(2):
            places = []
            for k in range(2):
                at = turned(xyz, k)
                places.append((wrap(at[1] + OFF[s]), u_parts(at[0])[h]))
            rows = jnp.concatenate(
                [xv[k, places[k][0], places[k][1]].reshape(128, D) for k in range(2)], axis=0
            )
            both = jnp.dot(rows, wgu[...], preferred_element_type=F32)
            gate, up = both[:, :FF], both[:, FF:]
            hidden = (gate / (1.0 + jnp.exp(-gate)) * up).astype(BF)
            result = jnp.dot(hidden, wd[...], preferred_element_type=F32).astype(BF)
            for g in range(3):
                at, width = COLS[g]
                for k in range(2):
                    sent[g][k, places[k][0], places[k][1]] = result[
                        k * 128:k * 128 + 128, at:at + width
                    ].reshape(2, 4, CAP, width)
            for dc in (2, 1, 3, 0):
                for dk in (0, 1):
                    third(0, s, h, dc, dk).start()
            for dk in (0, 1):
                third(2, s, h, OFF[s], dk).start()
            for dk in (0, 1):
                u = turned(xyz, core if dk == 0 else 1 - core)[0]
                if h == 0:
                    away = 2 * (1 - lax.div(u, 2)) - u
                    dcs = [away, away + 1]
                else:
                    dcs = [1 - 2 * lax.rem(u, 2), 0]
                for dc in dcs:
                    third(1, s, h, dc, dk).start()
        if s == 2:
            received(0, 0)
            combine(0, 2)
    for s in range(4):
        for g in (1, 2):
            received(g, s)
    combine(1, 2)
    combine(2, 2)
    received(0, 1)
    for g in range(3):
        combine_near(g, 0)
    received(0, 2)
    for g in range(3):
        combine_near(g, 1)
    for g in range(3):
        for direction in range(2):
            half(g, direction).wait_recv()

    def added(i, carry):
        for g in range(3):
            for direction in range(2):
                combine_on(g, direction, i)
        return carry

    lax.fori_loop(0, 2, added, 0)
    received(0, 3)
    for g in range(3):
        combine(g, 0)
        for brel in (2, 1, 3):
            pool_second(g, brel).start()
    for copy in load_bank:
        copy.start()
    for copy in load_bank:
        copy.wait()

    def norm(i, carry):
        total = jnp.zeros((128, 1), F32)
        for g in range(3):
            wide = back[g][lax.div(i, 4), lax.rem(i, 4)].reshape(128, COLS[g][1]).astype(F32)
            total += jnp.sum(wide * wide, axis=1, keepdims=True)
        norms[i] = jnp.broadcast_to(total, (128, 128))
        return carry

    lax.fori_loop(0, 16, norm, 0)

    for g in range(3):
        a_axis, b_axis, _ = ORDER[g]
        b = uvw[b_axis]
        for brel in (1, 2, 3):
            pool_second(g, brel).wait_recv()
        for arel in (2, 1, 3, 0):
            a = wrap(uvw[a_axis] + arel)
            total = pools[g][b, a].astype(F32)
            for i in range(3):
                total += pools2[g][i, a].astype(F32)
            if arel:
                pools[g][b, a] = total.astype(BF)
                pool_first(g, arel).start()
            else:
                summed[:, spans[g]] = total
    for g in range(3):
        for arel in (1, 2, 3):
            pool_first(g, arel).wait_recv()
        total = summed[:, spans[g]]
        for i in range(3):
            total += pools1[g][i].astype(F32)
        summed[:, spans[g]] = total
    whole_sum = summed[...]
    pooled = (
        whole_sum * lax.rsqrt(jnp.sum(whole_sum * whole_sum, axis=1, keepdims=True) + 1e-06)
    ).astype(BF)
    docs[center] = pooled

    def gather(i):
        return remote(docs.at[center], docs.at[center], gs.at[i], gr.at[i], mates[i])

    def tell(i):
        return remote(best, near.at[center], ns.at[i], nr.at[i], mates[i])

    for i in range(15):
        gather(i).start()
    wide = pooled.astype(F32)
    own = jnp.sum(wide * wide, axis=1, keepdims=True)
    lane = lax.broadcasted_iota(jnp.int32, (DOC_DEV, 128), 1)
    sub = lax.broadcasted_iota(jnp.int32, (DOC_DEV, 128), 0)
    own = jnp.sum(jnp.where(lane == center * DOC_DEV + sub, own, 0.0), axis=0, keepdims=True)
    def settle(i, carry):
        for g in range(3):
            a_axis, b_axis, _ = ORDER[g]
            b = uvw[b_axis]
            for direction in range(2):
                a = 2 * direction + i
                second(g, 0, a).wait_recv()
                second(g, 1, a).wait_recv()
                total = part[g][b, a].astype(F32)
                for j in range(2):
                    total += sums[g][j, a].astype(F32)
                arel = wrap(a - uvw[a_axis])

                @pl.when(arel == 0)
                def _(g=g, total=total):
                    comb[:, spans[g]] = total

                @pl.when(arel != 0)
                def _(g=g, b=b, a=a, total=total, arel=arel):
                    part[g][b, a] = total.astype(BF)
                    first(g, arel).start()
        return carry

    lax.fori_loop(0, 2, settle, 0)
    for i in range(15):
        gather(i).wait_recv()
    block = docs[...].reshape(16 * DOC_DEV, D)

    def nearest_of(i, nearest):
        products = jnp.zeros((512, 128), F32)
        for g in range(3):
            at, width = COLS[g]
            products += lax.dot_general(
                back[g][i].reshape(512, width), block[:, at:at + width],
                (((1,), (1,)), ((), ())), preferred_element_type=F32,
            )
        distance = norms[pl.ds(i * 4, 4)].reshape(512, 128) - 2.0 * products
        return jnp.minimum(nearest, jnp.min(distance.reshape(64, 8, 128), axis=0))

    nearest = lax.fori_loop(0, 4, nearest_of, jnp.full((8, 128), jnp.inf, F32))
    best[...] = nearest
    near[center] = nearest
    for i in range(15):
        tell(i).start()
    for g in range(3):
        for arel in (1, 2, 3):
            first(g, arel).wait_recv()
        total = comb[:, spans[g]]
        for i in range(3):
            total += last[g][i].astype(F32)
        out_ref[:, spans[g]] = total.astype(BF)
    for i in range(15):
        tell(i).wait_recv()
    closest = jnp.min(jnp.min(near[...], axis=0), axis=0, keepdims=True)
    mine = pltpu.roll(closest + own, lax.rem(128 - center * DOC_DEV, 128), 1)
    score_ref[...] = mine[:, 0:DOC_DEV]
    for g in range(3):
        for s in range(4):
            third_all(g, s).wait_send()
        for direction in range(2):
            half(g, direction).wait_send()
            for a in range(4):
                second(g, direction, a).wait_send()
        for d in (1, 2, 3):
            first(g, d).wait_send()
            pool_second(g, d).wait_send()
            pool_first(g, d).wait_send()
    for i in range(15):
        gather(i).wait_send()
        tell(i).wait_send()


def layer(tokens, ids, gates, doc_ids, wgu, wd, bank):
    any_spec, vmem = pl.BlockSpec(memory_space=pl.ANY), pl.BlockSpec(memory_space=pltpu.VMEM)
    dma = pltpu.SemaphoreType.DMA
    return pl.pallas_call(
        layer_kernel,
        out_shape=[
            jax.ShapeDtypeStruct((TOK, D), BF),
            jax.ShapeDtypeStruct((1, DOC_DEV), F32),
        ],
        in_specs=[vmem] * 4 + [any_spec] * 3,
        out_specs=[vmem] * 2,
        scratch_shapes=[
            pltpu.VMEM((3, 4, 4, 24, TOK), F32),
            pltpu.VMEM((3, 4, 4, 16, TOK), F32),
            pltpu.VMEM((TOK, TOK), BF),
            pltpu.VMEM((3, 4, 4, TOK + 16, 2 * TOK), BF),
        ]
        + [pltpu.VMEM((4, 4, TOK, w), BF) for _, w in COLS]
        + [pltpu.VMEM((2, 4, 4, 4, CAP, w), BF) for _, w in COLS]
        + [
            pltpu.VMEM((D, 2 * FF), BF),
            pltpu.VMEM((FF, D), BF),
            pltpu.VMEM((2, 4, 4, 4, CAP, D), BF),
        ]
        + [pltpu.VMEM((4, 4, 8, CAP, w), BF) for _, w in COLS]
        + [pltpu.VMEM((2, 2, TOK, w), BF) for _, w in COLS]
        + [pltpu.VMEM((2, 4, TOK, w), BF) for _, w in COLS]
        + [pltpu.VMEM((3, TOK, w), BF) for _, w in COLS]
        + [
            pltpu.VMEM((TOK, D), F32),
            pltpu.VMEM((16, DOC_DEV, D), BF),
            pltpu.VMEM((8, 128), F32),
            pltpu.VMEM((16, 8, 128), F32),
            pltpu.VMEM((16, 128, 128), F32),
        ]
        + [pltpu.VMEM((4, 4, DOC_DEV, w), BF) for _, w in COLS]
        + [pltpu.VMEM((3, 4, DOC_DEV, w), BF) for _, w in COLS]
        + [pltpu.VMEM((3, DOC_DEV, w), BF) for _, w in COLS]
        + [pltpu.VMEM((DOC_DEV, D), F32)]
        + [dma((3, 3)), dma((3, 3)), dma((3, 2, 4)), dma((3, 2, 4)), dma((3, 4)), dma((3, 4))]
        + [dma((3, 3))] * 4
        + [dma((3,)), dma((3,)), dma((3, 4))]
        + [dma((2,)), dma((3,))]
        + [dma((3, 4))] * 3
        + [dma((3, 2))] * 2
        + [dma((3, 2, 4))] * 2
        + [dma((3, 3))] * 6
        + [dma((15,))] * 4,
        compiler_params=pltpu.CompilerParams(
            collective_id=0, has_side_effects=True, vmem_limit_bytes=63 << 20
        ),
        name="layer",
    )(tokens, ids, gates, doc_ids, wgu, wd, bank)


def finish_kernel(rows_ref, score_ref, out_ref, own_ref):
    out_ref[...] = rows_ref[...]
    own_ref[...] = score_ref[...]


def finish(rows, scores):
    return pl.pallas_call(
        finish_kernel,
        out_shape=[
            jax.ShapeDtypeStruct((TOK, D), BF),
            jax.ShapeDtypeStruct((1, DOC_DEV), F32),
        ],
        name="finish",
    )(rows, scores)


def local(tokens, doc_ids, expert_ids, gate_raw, gate_up, down, bank):
    layer_out, scores = layer(
        tokens, expert_ids.T, gate_raw.T, doc_ids, gate_up[0], down[0],
        bank.reshape(4, 4, 8, CAP, D),
    )
    layer_out, scores = finish(layer_out, scores)
    return layer_out, scores.reshape(DOC_DEV)


def solution(mesh):
    return jax.shard_map(
        local,
        mesh=mesh,
        in_specs=(
            P(("center", "expert"), None),
            P(("center", "expert"), None),
            P(("center", "expert"), None),
            P(("center", "expert"), None),
            P(("center", "expert"), None, None),
            P(("center", "expert"), None, None),
            P("center", None),
        ),
        out_specs=(P(("center", "expert"), None), P(("center", "expert"))),
        check_vma=False,
    )
```

```python
import functools

import jax
import jax.numpy as jnp
from jax import lax
from jax.experimental import pallas as pl
from jax.experimental.pallas import tpu as pltpu
from jax.sharding import PartitionSpec as P

MESH = pl.DeviceIdType.MESH
D = 2048
FF = 768
TOK = 128
CAP = 16
DOC_DEV = 8
COLS = ((0, 768), (768, 640), (1408, 640))
ORDER = ((0, 1, 2), (1, 2, 0), (2, 0, 1))
BF = jnp.bfloat16
F32 = jnp.float32


def where_am_i():
    center = lax.axis_index("center")
    expert = lax.axis_index("expert")
    return (lax.rem(center, 4), lax.div(center, 4), lax.div(expert, 2)), lax.rem(expert, 2)


def wrap(v):
    return lax.rem(v + 4, 4)


def turned(xyz, k):
    x, y, z = xyz
    return (x + k * (y - x), y + k * (z - y), z + k * (x - z))


def straight(uvw, k):
    u, v, w = uvw
    return (u + k * (w - u), v + k * (u - v), w + k * (v - w))


def real_device(xyz, core):
    return (xyz[1] * 4 + xyz[0], xyz[2] * 2 + core)


def device_at(uvw, k, core):
    return real_device(straight(uvw, k), core)


def moved(uvw, axis, delta):
    out = list(uvw)
    out[axis] = wrap(out[axis] + delta)
    return tuple(out)


def enter(peers):
    barrier = pltpu.get_barrier_semaphore()
    for peer in peers:
        pl.semaphore_signal(barrier, 1, device_id=peer, device_id_type=MESH)
    return lambda: pl.semaphore_wait(barrier, len(peers))


def line_peers(xyz, core):
    peers = [real_device(xyz, 1 - core)]
    for axis in range(3):
        for delta in (1, 2, 3):
            for other in (core, 1 - core):
                peers.append(real_device(moved(xyz, axis, delta), other))
    return peers


def remote(src, dst, send, recv, dev):
    return pltpu.make_async_remote_copy(
        src_ref=src, dst_ref=dst, send_sem=send, recv_sem=recv, device_id=dev, device_id_type=MESH
    )


def rows_of(ref, g, b, c, core):
    cols = pl.ds(*COLS[g])
    if g == 0:
        return ref.at[core, b, :, c, :, cols]
    if g == 1:
        return ref.at[core, :, c, b, :, cols]
    return ref.at[core, c, b, :, :, cols]


def expert_number(g, uvw, core, k, c):
    at = list(uvw)
    at[ORDER[g][2]] = c
    x, y, z = straight(at, core)
    return (y * 4 + x) * 8 + z * 2 + k


R_TO_DELTA = (0, 1, 3, 2)
BREL = (0, 3, 1, 2)

OFF = (2, 1, 3, 0)


def layer_kernel(
    tok_ref, ids_ref, gate_ref, doc_ref, wgu_hbm, wd_hbm, bank_hbm,
    out_ref, score_ref,
    m_ref, qg_ref, tri_ref, cw_ref, h0, h1, h2, s0, s1, s2,
    wgu, wd, xv, r30, r31, r32, f0, f1, f2, r20, r21, r22, r10, r11, r12,
    comb, docs, best, near, norms, q0, q1, q2, q20, q21, q22, q10, q11, q12, summed,
    p1s, p1r, p2s, p2r, fs, fr, m1s, m1r, m2s, m2r, ps, pr, loc1,
    wsem, bsem, c3s, c3r, loc, hs, hr, c2s, c2r, c1s, c1r, d2s, d2r, d1s, d1r, gs, gr, ns, nr,
):
    xyz, core = where_am_i()
    x, y, z = xyz
    uvw = turned(xyz, core)
    center = lax.axis_index("center")
    back, held, sent = (r30, r31, r32), (h0, h1, h2), (s0, s1, s2)
    part = held
    halves, sums, last = (f0, f1, f2), (r20, r21, r22), (r10, r11, r12)
    pools, pools2, pools1 = (q0, q1, q2), (q20, q21, q22), (q10, q11, q12)
    spans = [pl.ds(at, width) for at, width in COLS]
    plane = [(dx, dy) for dy in range(4) for dx in range(4) if dx or dy]
    mates = [real_device((wrap(x + dx), wrap(y + dy), z), core) for dx, dy in plane]
    ready = enter(
        line_peers(xyz, core) + [m for m, (dx, dy) in zip(mates, plane) if dx and dy]
    )
    load_w = [
        pltpu.make_async_copy(wgu_hbm, wgu, wsem.at[0]),
        pltpu.make_async_copy(wd_hbm, wd, wsem.at[1]),
    ]
    for q in range(4):
        rows = pl.ds(q * 32, 32)
        values = tok_ref[rows, :].astype(F32)
        scale = lax.rsqrt(jnp.mean(values * values, axis=-1, keepdims=True) + 1e-06)
        normed = (values * scale).astype(BF)
        for g in range(3):
            a, b = uvw[ORDER[g][0]], uvw[ORDER[g][1]]
            held[g][b, a, rows, :] = normed[:, COLS[g][0]:COLS[g][0] + COLS[g][1]]
    gates = gate_ref[...]
    gates = gates / jnp.sum(gates, axis=0, keepdims=True)
    ids = ids_ref[...].astype(F32)
    for g in range(3):
        a, b = uvw[ORDER[g][0]], uvw[ORDER[g][1]]
        m_ref[g, b, a, 0:8, :] = ids
        m_ref[g, b, a, 8:16, :] = gates
        m_ref[g, b, a, 16:24, :] = jnp.broadcast_to(doc_ref[...].astype(F32), (8, TOK))
    earlier = lax.broadcasted_iota(jnp.int32, (TOK, TOK), 0)
    later = lax.broadcasted_iota(jnp.int32, (TOK, TOK), 1)
    tri_ref[...] = jnp.where(earlier < later, 1.0, 0.0).astype(BF)
    ready()
    for copy in load_w:
        copy.start()

    def along(g, which, delta):
        return device_at(moved(uvw, ORDER[g][which], delta), core, core)

    def meta1(g, d):
        a, b = uvw[ORDER[g][0]], uvw[ORDER[g][1]]
        blk = m_ref.at[g, b, a]
        return remote(blk, blk, m1s.at[g, d - 1], m1r.at[g, d - 1], along(g, 0, d))

    def meta2(g, d):
        b = uvw[ORDER[g][1]]
        blk = m_ref.at[g, b]
        return remote(blk, blk, m2s.at[g, d - 1], m2r.at[g, d - 1], along(g, 1, d))

    def spread1(g, d):
        a, b = uvw[ORDER[g][0]], uvw[ORDER[g][1]]
        blk = held[g].at[b, a]
        return remote(blk, blk, p1s.at[g, d - 1], p1r.at[g, d - 1], along(g, 0, d))

    def opposite(g, side):
        a, b = uvw[ORDER[g][0]], uvw[ORDER[g][1]]
        blk = held[g].at[b, wrap(a + (3 if side == 0 else 1)), side * 64:side * 64 + 64]
        return remote(
            blk, blk, p1s.at[g, 1], p1r.at[g, 1], along(g, 0, 1 if side == 0 else 3)
        )

    def spread2(g, direction, r):
        a, b = uvw[ORDER[g][0]], uvw[ORDER[g][1]]
        blk = held[g].at[b, wrap(a - R_TO_DELTA[r])]
        return remote(
            blk, blk, p2s.at[g, direction, r], p2r.at[g, direction, r],
            along(g, 1, 1 if direction == 0 else 3),
        )

    def onward(g, r):
        a, b = uvw[ORDER[g][0]], uvw[ORDER[g][1]]
        direction = r % 2
        blk = held[g].at[wrap(b + (3 if direction == 0 else 1)), wrap(a - R_TO_DELTA[r])]
        return remote(
            blk, blk, fs.at[g, r], fr.at[g, r], along(g, 1, 1 if direction == 0 else 3)
        )

    for g in range(3):
        for d in (1, 3, 2):
            meta1(g, d).start()
    for g in range(3):
        for d in (1, 3):
            spread1(g, d).start()
    for g in range(3):
        for direction in range(2):
            spread2(g, direction, 0).start()
    for g in range(3):
        for d in (1, 3, 2):
            meta1(g, d).wait_recv()
        for d in (1, 3, 2):
            meta2(g, d).start()
    for r in (1, 2, 3):
        for g in range(3):
            spread1(g, R_TO_DELTA[r]).wait_recv()
            if r < 3:
                opposite(g, r - 1).start()
            for direction in range(2):
                spread2(g, direction, r).start()

    def select(g, brel):
        a_axis, b_axis, c_axis = ORDER[g]
        b = wrap(uvw[b_axis] + brel)
        ids = m_ref[g, b, :, 0:8, :]
        gates = m_ref[g, b, :, 8:16, :]
        sub = lax.broadcasted_iota(jnp.int32, (4, 8, TOK), 1)
        named = jnp.zeros((4, 8, TOK), F32)
        gated = jnp.zeros((4, 8, TOK), F32)
        for j in range(8):
            number = expert_number(g, uvw, core, j // 4, j % 4).astype(F32)
            hit = ids == number
            named = jnp.where(sub == j, jnp.sum(jnp.where(hit, 1.0, 0.0), axis=1, keepdims=True), named)
            gated = jnp.where(sub == j, jnp.sum(jnp.where(hit, gates, 0.0), axis=1, keepdims=True), gated)
        before = jnp.dot(
            named.reshape(32, TOK).astype(BF), tri_ref[...], preferred_element_type=F32
        ).reshape(4, 8, TOK)
        qg_ref[g, b, :, 0:8, :] = jnp.where(named > 0.5, before, -1.0)
        qg_ref[g, b, :, 8:16, :] = gated
        slot = lax.broadcasted_iota(jnp.int32, (8, CAP, TOK), 1).astype(F32)

        def body(a, carry):
            place = qg_ref[g, b, a, 0:8, :]
            pick = jnp.where(place[:, None, :] == slot, 1.0, 0.0).reshape(8 * CAP, TOK).astype(BF)
            rows = jnp.dot(pick, held[g][b, a], preferred_element_type=F32).astype(BF)
            sent[g][:, brel, a] = rows.reshape(2, 4, CAP, COLS[g][1])
            return carry

        lax.fori_loop(0, 4, body, 0)

    def rows_out(g, brel, dc, dk):
        c_axis = ORDER[g][2]
        c, b = uvw[c_axis], wrap(uvw[ORDER[g][1]] + brel)
        target, other = wrap(c + dc), (core if dk == 0 else 1 - core)
        src = sent[g].at[other, brel, :, target]
        dst = rows_of(xv, g, b, c, core)
        if dc == 0 and dk == 0:
            return pltpu.make_async_copy(src, dst, loc1.at[g, brel])
        return remote(src, dst, ps.at[g], pr.at[g], device_at(moved(uvw, c_axis, dc), core, other))

    def send_rows(g, brel):
        for dc in (2, 1, 3, 0):
            for dk in (0, 1):
                rows_out(g, brel, dc, dk).start()

    for g in range(3):
        select(g, 0)
        send_rows(g, 0)
    for r in range(4):
        for g in range(3):
            spread2(g, r % 2, r).wait_recv()
            onward(g, r).start()
    for g in range(3):
        for d in (1, 3, 2):
            meta2(g, d).wait_recv()
    for direction, brel in ((0, 3), (1, 1)):
        for g in range(3):
            for r in range(4):
                if r % 2 != direction:
                    spread2(g, direction, r).wait_recv()
            select(g, brel)
            send_rows(g, brel)
    for g in range(3):
        for r in range(4):
            onward(g, r).wait_recv()
        select(g, 2)
        send_rows(g, 2)
    def weigh(i, carry):
        b, a = lax.div(i, 4), lax.rem(i, 4)
        for g in range(3):
            place, gate = qg_ref[g, b, a, 0:8, :], qg_ref[g, b, a, 8:16, :]
            slots = lax.broadcasted_iota(jnp.int32, (8, CAP, TOK), 1).astype(F32)
            weight = jnp.where(place[:, None, :] == slots, gate[:, None, :], 0.0)
            weight = weight.reshape(8 * CAP, TOK).T
            high = weight.astype(BF)
            low = (weight - high.astype(F32)).astype(BF)
            cw_ref[g, b, a, 0:TOK, 0:TOK] = high
            cw_ref[g, b, a, 0:TOK, TOK:2 * TOK] = low
            number = lax.broadcasted_iota(jnp.int32, (16, TOK), 0).astype(F32)
            member = jnp.where(m_ref[g, b, a, 16:17, :] == number, 1.0, 0.0).astype(BF)
            pool = jnp.dot(member, high, preferred_element_type=F32)
            pool += jnp.dot(member, low, preferred_element_type=F32)
            high = pool.astype(BF)
            cw_ref[g, b, a, TOK:TOK + 16, 0:TOK] = high
            cw_ref[g, b, a, TOK:TOK + 16, TOK:2 * TOK] = (pool - high.astype(F32)).astype(BF)
        return carry

    lax.fori_loop(0, 16, weigh, 0)
    for g in range(3):
        for d in (1, 2, 3):
            meta1(g, d).wait_send()
            meta2(g, d).wait_send()
            spread1(g, d).wait_send()
        for r in range(4):
            onward(g, r).wait_send()
            for direction in range(2):
                spread2(g, direction, r).wait_send()
        for brel in range(4):
            rows_out(g, brel, 0, 0).wait()
        whole = remote(
            back[g].at[:, :, 0:7], back[g].at[:, :, 0:7], ps.at[g], pr.at[g],
            real_device(xyz, 1 - core),
        )
        whole.wait_send()
        whole.wait_recv()

    load_bank = [
        pltpu.make_async_copy(bank_hbm.at[:, :, :, :, spans[g]], back[g], bsem.at[g])
        for g in range(3)
    ]

    def third(g, s, h, dc, dk):
        other = core if dk == 0 else 1 - core
        at = turned(xyz, other)
        axis = ORDER[g][2]
        row, part_u = wrap(at[1] + OFF[s]), u_parts(at[0])[h]
        mine = core * 4 + at[axis]
        target = wrap(at[axis] + dc)
        if g == 0:
            src, dst = sent[0].at[other, row, part_u, target], back[0].at[row, part_u, mine]
        elif g == 1:
            src, dst = sent[1].at[other, row, target], back[1].at[:, row, mine]
        else:
            src, dst = sent[2].at[other, row, part_u], back[2].at[part_u, :, mine]
        if type(dc) is int and dc == 0 and dk == 0:
            return pltpu.make_async_copy(src, dst, loc.at[g, s])
        return remote(
            src, dst, c3s.at[g, s], c3r.at[g, s], device_at(moved(at, axis, dc), other, other)
        )

    def u_parts(u):
        own_half = lax.div(u, 2)
        return (pl.ds(2 * (1 - own_half), 2), pl.ds(2 * own_half, 2))

    def third_all(g, s):
        row = wrap(uvw[1] + OFF[s])
        if g == 0:
            blk = back[0].at[row, :, 0:7]
        elif g == 1:
            blk = back[1].at[:, row, 0:7]
        else:
            blk = back[2].at[:, :, 0:(2 if s < 3 else 1)]
        return remote(blk, blk, c3s.at[g, s], c3r.at[g, s], real_device(xyz, 1 - core))

    def half(g, direction):
        a0 = 2 * direction
        return remote(
            part[g].at[wrap(uvw[ORDER[g][1]] + 2), a0:a0 + 2], halves[g].at[direction],
            hs.at[g, direction], hr.at[g, direction],
            device_at(moved(uvw, ORDER[g][1], 1 if direction == 0 else 3), core, core),
        )

    def second(g, direction, a):
        step = 1 if direction == 0 else 3
        return remote(
            part[g].at[wrap(uvw[ORDER[g][1]] + step), a], sums[g].at[direction, a],
            c2s.at[g, direction, a], c2r.at[g, direction, a],
            device_at(moved(uvw, ORDER[g][1], step), core, core),
        )

    def first(g, arel):
        a_axis, b_axis, _ = ORDER[g]
        return remote(
            part[g].at[uvw[b_axis], wrap(uvw[a_axis] + arel)], last[g].at[arel - 1],
            c1s.at[g, arel - 1], c1r.at[g, arel - 1],
            device_at(moved(uvw, a_axis, arel), core, core),
        )

    def total_of(g, b, a):
        rows = back[g][b, a].reshape(8 * CAP, COLS[g][1])
        total = jnp.dot(
            cw_ref[g, b, a], jnp.concatenate([rows, rows], axis=0), preferred_element_type=F32
        )
        pools[g][b, a] = total[TOK:TOK + DOC_DEV].astype(BF)
        return total[0:TOK]

    def pool_second(g, brel):
        b_axis = ORDER[g][1]
        return remote(
            pools[g].at[wrap(uvw[b_axis] + brel)], pools2[g].at[brel - 1],
            d2s.at[g, brel - 1], d2r.at[g, brel - 1],
            device_at(moved(uvw, b_axis, brel), core, core),
        )

    def pool_first(g, arel):
        a_axis, b_axis, _ = ORDER[g]
        return remote(
            pools[g].at[uvw[b_axis], wrap(uvw[a_axis] + arel)], pools1[g].at[arel - 1],
            d1s.at[g, arel - 1], d1r.at[g, arel - 1],
            device_at(moved(uvw, a_axis, arel), core, core),
        )

    def combine(g, brel):
        b = wrap(uvw[ORDER[g][1]] + brel)

        def plain(a, carry):
            part[g][b, a] = total_of(g, b, a).astype(BF)
            return carry

        lax.fori_loop(0, 4, plain, 0)
        if brel == 2:
            half(g, 0).start()
            half(g, 1).start()

    def combine_near(g, direction):
        b = wrap(uvw[ORDER[g][1]] + (1 if direction == 0 else 3))

        def plain(a, carry):
            part[g][b, a] = total_of(g, b, a).astype(BF)
            second(g, direction, a).start()
            return carry

        a0 = 2 - 2 * direction
        lax.fori_loop(a0, a0 + 2, plain, 0)

    def combine_far(g, direction):
        b = wrap(uvw[ORDER[g][1]] + (1 if direction == 0 else 3))

        def plain(a, carry):
            part[g][b, a] = total_of(g, b, a).astype(BF)
            return carry

        lax.fori_loop(2 * direction, 2 * direction + 2, plain, 0)

    def send_on(i):
        for g in range(3):
            for direction in range(2):
                b = wrap(uvw[ORDER[g][1]] + (1 if direction == 0 else 3))
                a = 2 * direction + i
                total = part[g][b, a].astype(F32) + halves[g][direction, i].astype(F32)
                part[g][b, a] = total.astype(BF)
                second(g, direction, a).start()

    def received(g, s):
        if g == 0:
            for h in range(2):
                third(0, s, h, 0, 0).wait()
        elif g == 1:
            third(1, s, 1, 0, 0).wait()
        elif s == 3:
            for h in range(2):
                third(2, s, h, 0, 0).wait()
        third_all(g, s).wait_recv()

    for s in range(4):
        if s == 0:
            for copy in load_w:
                copy.wait()
        for h in range(2):
            places = []
            for k in range(2):
                at = turned(xyz, k)
                places.append((wrap(at[1] + OFF[s]), u_parts(at[0])[h]))
            rows = jnp.concatenate(
                [xv[k, places[k][0], places[k][1]].reshape(128, D) for k in range(2)], axis=0
            )
            both = jnp.dot(rows, wgu[...], preferred_element_type=F32)
            gate, up = both[:, :FF], both[:, FF:]
            hidden = (gate / (1.0 + jnp.exp(-gate)) * up).astype(BF)
            result = jnp.dot(hidden, wd[...], preferred_element_type=F32).astype(BF)
            for g in range(3):
                at, width = COLS[g]
                for k in range(2):
                    sent[g][k, places[k][0], places[k][1]] = result[
                        k * 128:k * 128 + 128, at:at + width
                    ].reshape(2, 4, CAP, width)
            for dc in (2, 1, 3, 0):
                for dk in (0, 1):
                    third(0, s, h, dc, dk).start()
            for dk in (0, 1):
                third(2, s, h, OFF[s], dk).start()
            for dk in (0, 1):
                u = turned(xyz, core if dk == 0 else 1 - core)[0]
                if h == 0:
                    away = 2 * (1 - lax.div(u, 2)) - u
                    dcs = [away, away + 1]
                else:
                    dcs = [1 - 2 * lax.rem(u, 2), 0]
                for dc in dcs:
                    third(1, s, h, dc, dk).start()
        if s == 2:
            received(0, 0)
            combine(0, 2)
    for s in range(4):
        for g in (1, 2):
            received(g, s)
    combine(1, 2)
    combine(2, 2)
    received(0, 1)
    for g in range(3):
        combine_near(g, 0)
    received(0, 2)
    for g in range(3):
        combine_near(g, 1)
    received(0, 3)
    for g in range(3):
        combine_far(g, 0)
        combine_far(g, 1)
        combine(g, 0)
        for brel in (2, 1, 3):
            pool_second(g, brel).start()
    for g in range(3):
        for direction in range(2):
            half(g, direction).wait_recv()
    send_on(0)
    for copy in load_bank:
        copy.start()
    for copy in load_bank:
        copy.wait()

    def norm(i, carry):
        total = jnp.zeros((128, 1), F32)
        for g in range(3):
            wide = back[g][lax.div(i, 4), lax.rem(i, 4)].reshape(128, COLS[g][1]).astype(F32)
            total += jnp.sum(wide * wide, axis=1, keepdims=True)
        norms[i] = jnp.broadcast_to(total, (128, 128))
        return carry

    lax.fori_loop(0, 16, norm, 0)

    for g in range(3):
        a_axis, b_axis, _ = ORDER[g]
        b = uvw[b_axis]
        for brel in (1, 2, 3):
            pool_second(g, brel).wait_recv()
        for arel in (2, 1, 3, 0):
            a = wrap(uvw[a_axis] + arel)
            total = pools[g][b, a].astype(F32)
            for i in range(3):
                total += pools2[g][i, a].astype(F32)
            if arel:
                pools[g][b, a] = total.astype(BF)
                pool_first(g, arel).start()
            else:
                summed[:, spans[g]] = total
    send_on(1)
    for g in range(3):
        for arel in (1, 2, 3):
            pool_first(g, arel).wait_recv()
        total = summed[:, spans[g]]
        for i in range(3):
            total += pools1[g][i].astype(F32)
        summed[:, spans[g]] = total
    whole_sum = summed[...]
    pooled = (
        whole_sum * lax.rsqrt(jnp.sum(whole_sum * whole_sum, axis=1, keepdims=True) + 1e-06)
    ).astype(BF)
    docs[center] = pooled

    def gather(i):
        return remote(docs.at[center], docs.at[center], gs.at[i], gr.at[i], mates[i])

    def tell(i):
        return remote(best, near.at[center], ns.at[i], nr.at[i], mates[i])

    for i in range(15):
        gather(i).start()
    wide = pooled.astype(F32)
    own = jnp.sum(wide * wide, axis=1, keepdims=True)
    lane = lax.broadcasted_iota(jnp.int32, (DOC_DEV, 128), 1)
    sub = lax.broadcasted_iota(jnp.int32, (DOC_DEV, 128), 0)
    own = jnp.sum(jnp.where(lane == center * DOC_DEV + sub, own, 0.0), axis=0, keepdims=True)
    def settle(i, carry):
        for g in range(3):
            a_axis, b_axis, _ = ORDER[g]
            b = uvw[b_axis]
            for direction in range(2):
                a = 2 * direction + i
                second(g, 0, a).wait_recv()
                second(g, 1, a).wait_recv()
                total = part[g][b, a].astype(F32)
                for j in range(2):
                    total += sums[g][j, a].astype(F32)
                arel = wrap(a - uvw[a_axis])

                @pl.when(arel == 0)
                def _(g=g, total=total):
                    comb[:, spans[g]] = total

                @pl.when(arel != 0)
                def _(g=g, b=b, a=a, total=total, arel=arel):
                    part[g][b, a] = total.astype(BF)
                    first(g, arel).start()
        return carry

    lax.fori_loop(0, 2, settle, 0)
    for i in range(15):
        gather(i).wait_recv()
    block = docs[...].reshape(16 * DOC_DEV, D)

    def nearest_of(i, nearest):
        products = jnp.zeros((512, 128), F32)
        for g in range(3):
            at, width = COLS[g]
            products += lax.dot_general(
                back[g][i].reshape(512, width), block[:, at:at + width],
                (((1,), (1,)), ((), ())), preferred_element_type=F32,
            )
        distance = norms[pl.ds(i * 4, 4)].reshape(512, 128) - 2.0 * products
        return jnp.minimum(nearest, jnp.min(distance.reshape(64, 8, 128), axis=0))

    nearest = lax.fori_loop(0, 4, nearest_of, jnp.full((8, 128), jnp.inf, F32))
    best[...] = nearest
    near[center] = nearest
    for i in range(15):
        tell(i).start()
    for g in range(3):
        for arel in (1, 2, 3):
            first(g, arel).wait_recv()
        total = comb[:, spans[g]]
        for i in range(3):
            total += last[g][i].astype(F32)
        out_ref[:, spans[g]] = total.astype(BF)
    for i in range(15):
        tell(i).wait_recv()
    closest = jnp.min(jnp.min(near[...], axis=0), axis=0, keepdims=True)
    mine = pltpu.roll(closest + own, lax.rem(128 - center * DOC_DEV, 128), 1)
    score_ref[...] = mine[:, 0:DOC_DEV]
    for g in range(3):
        for s in range(4):
            third_all(g, s).wait_send()
        for direction in range(2):
            half(g, direction).wait_send()
            for a in range(4):
                second(g, direction, a).wait_send()
        for d in (1, 2, 3):
            first(g, d).wait_send()
            pool_second(g, d).wait_send()
            pool_first(g, d).wait_send()
    for i in range(15):
        gather(i).wait_send()
        tell(i).wait_send()


def layer(tokens, ids, gates, doc_ids, wgu, wd, bank):
    any_spec, vmem = pl.BlockSpec(memory_space=pl.ANY), pl.BlockSpec(memory_space=pltpu.VMEM)
    dma = pltpu.SemaphoreType.DMA
    return pl.pallas_call(
        layer_kernel,
        out_shape=[
            jax.ShapeDtypeStruct((TOK, D), BF),
            jax.ShapeDtypeStruct((1, DOC_DEV), F32),
        ],
        in_specs=[vmem] * 4 + [any_spec] * 3,
        out_specs=[vmem] * 2,
        scratch_shapes=[
            pltpu.VMEM((3, 4, 4, 24, TOK), F32),
            pltpu.VMEM((3, 4, 4, 16, TOK), F32),
            pltpu.VMEM((TOK, TOK), BF),
            pltpu.VMEM((3, 4, 4, TOK + 16, 2 * TOK), BF),
        ]
        + [pltpu.VMEM((4, 4, TOK, w), BF) for _, w in COLS]
        + [pltpu.VMEM((2, 4, 4, 4, CAP, w), BF) for _, w in COLS]
        + [
            pltpu.VMEM((D, 2 * FF), BF),
            pltpu.VMEM((FF, D), BF),
            pltpu.VMEM((2, 4, 4, 4, CAP, D), BF),
        ]
        + [pltpu.VMEM((4, 4, 8, CAP, w), BF) for _, w in COLS]
        + [pltpu.VMEM((2, 2, TOK, w), BF) for _, w in COLS]
        + [pltpu.VMEM((2, 4, TOK, w), BF) for _, w in COLS]
        + [pltpu.VMEM((3, TOK, w), BF) for _, w in COLS]
        + [
            pltpu.VMEM((TOK, D), F32),
            pltpu.VMEM((16, DOC_DEV, D), BF),
            pltpu.VMEM((8, 128), F32),
            pltpu.VMEM((16, 8, 128), F32),
            pltpu.VMEM((16, 128, 128), F32),
        ]
        + [pltpu.VMEM((4, 4, DOC_DEV, w), BF) for _, w in COLS]
        + [pltpu.VMEM((3, 4, DOC_DEV, w), BF) for _, w in COLS]
        + [pltpu.VMEM((3, DOC_DEV, w), BF) for _, w in COLS]
        + [pltpu.VMEM((DOC_DEV, D), F32)]
        + [dma((3, 3)), dma((3, 3)), dma((3, 2, 4)), dma((3, 2, 4)), dma((3, 4)), dma((3, 4))]
        + [dma((3, 3))] * 4
        + [dma((3,)), dma((3,)), dma((3, 4))]
        + [dma((2,)), dma((3,))]
        + [dma((3, 4))] * 3
        + [dma((3, 2))] * 2
        + [dma((3, 2, 4))] * 2
        + [dma((3, 3))] * 6
        + [dma((15,))] * 4,
        compiler_params=pltpu.CompilerParams(
            collective_id=0, has_side_effects=True, vmem_limit_bytes=63 << 20
        ),
        name="layer",
    )(tokens, ids, gates, doc_ids, wgu, wd, bank)


def finish_kernel(rows_ref, score_ref, out_ref, own_ref):
    out_ref[...] = rows_ref[...]
    own_ref[...] = score_ref[...]


def finish(rows, scores):
    return pl.pallas_call(
        finish_kernel,
        out_shape=[
            jax.ShapeDtypeStruct((TOK, D), BF),
            jax.ShapeDtypeStruct((1, DOC_DEV), F32),
        ],
        name="finish",
    )(rows, scores)


def local(tokens, doc_ids, expert_ids, gate_raw, gate_up, down, bank):
    layer_out, scores = layer(
        tokens, expert_ids.T, gate_raw.T, doc_ids, gate_up[0], down[0],
        bank.reshape(4, 4, 8, CAP, D),
    )
    layer_out, scores = finish(layer_out, scores)
    return layer_out, scores.reshape(DOC_DEV)


def solution(mesh):
    return jax.shard_map(
        local,
        mesh=mesh,
        in_specs=(
            P(("center", "expert"), None),
            P(("center", "expert"), None),
            P(("center", "expert"), None),
            P(("center", "expert"), None),
            P(("center", "expert"), None, None),
            P(("center", "expert"), None, None),
            P("center", None),
        ),
        out_specs=(P(("center", "expert"), None), P(("center", "expert"))),
        check_vma=False,
    )
```
